32 devices in a mesh: grp: 2 (over y), wa: 4 (over z), ta: 4 (over x, core).
Axes of the slice: x: 2, y: 2, z: 4, core: 2. Of those that a mesh axis runs over, the one named last changes fastest.
Arguments:
- node_features: float32 [8, 512, 1024], P(('grp', 'wa'), 'ta'), parts along dimension 0, may hold values from -21 to 21
- sensor_adjoint: float32 [8, 512, 1024], P(('grp', 'wa'), 'ta'), parts along dimension 0, may hold values from -6 to 6
- sensor_node: int32 [512], P('ta'), may hold values from 0 to 511, as said below
- neighbours: int32 [4, 2], replicated, may hold values from 0 to 3, as said below
- w_query: float32 [1024, 1024], P('wa', 'ta'), may hold values from -0.1875 to 0.1875
- w_key: float32 [1024, 1024], P('wa', 'ta'), may hold values from -0.1875 to 0.1875
- w_value: float32 [1024, 1024], P('wa', 'ta'), may hold values from -0.1875 to 0.1875
Outputs:
- input_adjoint: float32 [8, 512, 1024], P(('grp', 'wa'), 'ta'), parts along dimension 0
- query_weight_grad: float32 [2048, 1024], P(('grp', 'wa'), 'ta'), parts along dimension 0
- key_weight_grad: float32 [2048, 1024], P(('grp', 'wa'), 'ta'), parts along dimension 0
- value_weight_grad: float32 [2048, 1024], P(('grp', 'wa'), 'ta'), parts along dimension 0
The draws below stay inside these ranges and needn't reach their ends.
There are 2 independent parts, one for each index of `grp`. The reference program is written for one: setup_inputs(seed, part) draws one part's arguments, and reference() takes and returns one part's arrays. A program takes and returns all parts, laid end to end along the dimension named above; an argument that names none is the same for every part. Nothing has to cross between parts.
Inputs may be any that keep to these rules, and one draw needn't show every extreme that they name: `sensor_node`: each aligned block of 128 entries is a permutation of that block's node numbers. `neighbours`: each row names 2 different blocks.
All inputs are finite; a program needn't handle non-finite values.
Results may differ from the reference program's by a relative error of at most 0.0003.
Values sent between devices are 32-bit elements; how exact they have to be, the bound alone decides.
No kernel may reach another device: no remote copies, remote signals or barrier semaphores. Data moves between devices by JAX's collectives and lax.ppermute only.
A program may use at most 64 MiB of HBM per device.

```python
import jax
import jax.numpy as jnp
from jax import lax

D = 1024
DH = 64
BLOCK = 128
KB = 2
NODE_DEV = 128
NODES = 512
NB = 4
HOURS = 4


def draw_node_features(key, part):
    base_key = jax.random.fold_in(key, 11)
    return jnp.clip(jax.random.normal(base_key, (HOURS, NODES, D), jnp.float32), -4.0, 4.0)


def shuffle_nodes(subkey):
    return jax.random.permutation(subkey, NODE_DEV)


def draw_sensor_node(key, part):
    subkeys = jax.random.split(jax.random.fold_in(key, 21), NODES // NODE_DEV)
    shuffled = jax.vmap(shuffle_nodes)(subkeys).astype(jnp.int32)
    offsets = jnp.arange(NODES // NODE_DEV, dtype=jnp.int32)[:, None] * NODE_DEV
    return (shuffled + offsets).reshape(NODES).astype(jnp.int32)


def shuffle_blocks(subkey):
    return jax.random.permutation(subkey, NB)[:KB]


def draw_neighbours(key, part):
    subkeys = jax.random.split(jax.random.fold_in(key, 31), NB)
    return jax.vmap(shuffle_blocks)(subkeys).astype(jnp.int32)


def level_of(rng, dims, pieces, least, top_value):
    level = 1.0
    for axis_at, parts in pieces:
        steps = jax.random.uniform(jax.random.fold_in(jax.random.fold_in(rng, 6), axis_at), (parts,), jnp.float32, least / len(pieces), top_value / len(pieces))
        level = level * jnp.repeat(jnp.exp(steps), dims[axis_at] // parts).reshape((-1,) + (1,) * (len(dims) - 1 - axis_at))
    return level


def centred(rng, dims, spread, most, cuts=(), kind=jnp.bfloat16):
    values = spread * jax.random.normal(rng, dims, jnp.float32)
    if cuts:
        values = values * level_of(rng, dims, cuts, -0.22, 0.18)
    return jnp.clip(values, -most, most).astype(kind)


def setup_inputs(seed: int = 0, part: int = 0) -> dict:
    key_of = jax.random.split(jax.random.key(seed), 8)
    own_keys = jax.random.split(jax.random.fold_in(key_of[7], part), 8)
    node_features = draw_node_features(jax.random.fold_in(jax.random.fold_in(key_of[7], part), 71), part)
    sensor_adjoint = centred(own_keys[1], (HOURS, NODES, D), 1.0, 6.0, ((0, 4), (1, 4)), jnp.float32)
    sensor_node = draw_sensor_node(jax.random.fold_in(key_of[7], 71), part)
    neighbours = draw_neighbours(jax.random.fold_in(key_of[7], 71), part)
    w_query = centred(key_of[4], (D, D), D ** -0.5, 0.1875, ((0, 4), (1, 4)), jnp.float32)
    w_key = centred(key_of[5], (D, D), D ** -0.5, 0.1875, ((0, 4), (1, 4)), jnp.float32)
    w_value = centred(key_of[6], (D, D), D ** -0.5, 0.1875, ((0, 4), (1, 4)), jnp.float32)
    return dict(node_features=node_features, sensor_adjoint=sensor_adjoint, sensor_node=sensor_node, neighbours=neighbours, w_query=w_query, w_key=w_key, w_value=w_value)


def matmul(left, right):
    return jnp.dot(left, right, precision=lax.Precision.HIGHEST, preferred_element_type=jnp.float32)


def inner_rows(left, right):
    return lax.dot_general(left, right, (((0,), (0,)), ((), ())), precision=lax.Precision.HIGHEST, preferred_element_type=jnp.float32)


def block_attention_grads(query, key, value, adjoint, neighbours):
    node_count = query.shape[0]
    head_count = query.shape[1] // DH
    blocks = node_count // BLOCK
    highest = lax.Precision.HIGHEST
    score_scale = DH ** -0.5
    query_blocks = query.reshape(blocks, BLOCK, head_count, DH)
    grad_blocks = adjoint.reshape(blocks, BLOCK, head_count, DH)
    key_blocks = key.reshape(blocks, BLOCK, head_count, DH)[neighbours].reshape(blocks, KB * BLOCK, head_count, DH)
    value_blocks = value.reshape(blocks, BLOCK, head_count, DH)[neighbours].reshape(blocks, KB * BLOCK, head_count, DH)
    scores = jnp.einsum("bqhd,bkhd->bhqk", query_blocks, key_blocks, precision=highest) * score_scale
    attention = jax.nn.softmax(scores, axis=-1)
    attended = jnp.einsum("bhqk,bkhd->bqhd", attention, value_blocks, precision=highest)
    weight_adjoint = jnp.einsum("bqhd,bkhd->bhqk", grad_blocks, value_blocks, precision=highest)
    row_dots = jnp.einsum("bqhd,bqhd->bhq", grad_blocks, attended, precision=highest)
    score_adjoint = attention * (weight_adjoint - row_dots[..., None]) * score_scale
    query_adjoint = jnp.einsum("bhqk,bkhd->bqhd", score_adjoint, key_blocks, precision=highest)
    key_terms = jnp.einsum("bhqk,bqhd->bkhd", score_adjoint, query_blocks, precision=highest)
    value_terms = jnp.einsum("bhqk,bqhd->bkhd", attention, grad_blocks, precision=highest)
    selector = (neighbours[:, :, None] == jnp.arange(blocks, dtype=jnp.int32)[None, None, :]).astype(jnp.float32)
    key_adjoint = jnp.einsum("bjc,bjkhd->ckhd", selector, key_terms.reshape(blocks, KB, BLOCK, head_count, DH), precision=highest)
    value_adjoint = jnp.einsum("bjc,bjkhd->ckhd", selector, value_terms.reshape(blocks, KB, BLOCK, head_count, DH), precision=highest)
    return query_adjoint.reshape(node_count, -1), key_adjoint.reshape(node_count, -1), value_adjoint.reshape(node_count, -1)


def reference(node_features, sensor_adjoint, sensor_node, neighbours, w_query, w_key, w_value):
    def per_hour(running, inputs):
        hour_rows, readings = inputs
        adjoint = jnp.zeros_like(readings).at[sensor_node].set(readings)
        query = matmul(hour_rows, w_query)
        key = matmul(hour_rows, w_key)
        value = matmul(hour_rows, w_value)
        dquery, dkey_all, dvalue = block_attention_grads(query, key, value, adjoint, neighbours)
        back = matmul(dquery, w_query.T) + matmul(dkey_all, w_key.T) + matmul(dvalue, w_value.T)
        grad_query, grad_key, grad_value = running
        running = (grad_query + inner_rows(hour_rows, dquery), grad_key + inner_rows(hour_rows, dkey_all), grad_value + inner_rows(hour_rows, dvalue))
        return running, back

    initial = (jnp.zeros((D, D), jnp.float32), jnp.zeros((D, D), jnp.float32), jnp.zeros((D, D), jnp.float32))
    summed, input_adjoint = lax.scan(per_hour, initial, (node_features, sensor_adjoint))
    return (input_adjoint, summed[0], summed[1], summed[2])
```

```python
import functools

import jax
import jax.numpy as jnp
from jax import lax
from jax.experimental import pallas as pl
from jax.experimental.pallas import tpu as pltpu
from jax.sharding import PartitionSpec as P

DH = 64
BLOCK = 128
KB = 2
LANES = 128
F32 = jnp.float32
NN = ((1,), (0,))
NT = ((1,), (1,))
TN = ((0,), (0,))


def dot(left, right, dims):
    return lax.dot_general(
        left, right, (dims, ((), ())), precision=lax.Precision.HIGHEST, preferred_element_type=F32
    )


def local_call(body, outs, args, scalars=(), scratch=(), flops=0, vmem_mib=24):
    vmem = pl.BlockSpec(memory_space=pltpu.VMEM)
    smem = pl.BlockSpec(memory_space=pltpu.SMEM)
    moved = sum(4 * a.size for a in args) + sum(4 * o.size for o in outs)
    return pl.pallas_call(
        body,
        out_shape=outs,
        in_specs=[smem] * len(scalars) + [vmem] * len(args),
        out_specs=[vmem] * len(outs),
        scratch_shapes=scratch,
        cost_estimate=pl.CostEstimate(flops=flops, bytes_accessed=moved, transcendentals=0),
        compiler_params=pltpu.CompilerParams(vmem_limit_bytes=vmem_mib << 20),
    )(*scalars, *args)


def shaped(*shape):
    return jax.ShapeDtypeStruct(shape, F32)


def swap(value, axis, size, step):
    return lax.ppermute(value, axis, [(i, i ^ step) for i in range(size)])


def halves_body(chunks, wq, wk, wv, *outs):
    for c in range(chunks):
        cols = slice(c * LANES, (c + 1) * LANES)
        outs[c][:, 0:LANES] = wq[:, cols]
        outs[c][:, LANES : 2 * LANES] = wk[:, cols]
        outs[c][:, 2 * LANES : 3 * LANES] = wv[:, cols]


def weight_halves(info, w_query, w_key, w_value, rows, chunks):
    columns = w_query.shape[1]
    spec = pl.BlockSpec((rows, columns), lambda i, info: (info[1], 0))
    out = pl.BlockSpec((rows, 3 * LANES), lambda i, info: (0, 0))
    return pl.pallas_call(
        functools.partial(halves_body_prefetch, chunks),
        out_shape=[shaped(rows, 3 * LANES)] * chunks,
        grid_spec=pltpu.PrefetchScalarGridSpec(
            num_scalar_prefetch=1, grid=(1,), in_specs=[spec] * 3, out_specs=[out] * chunks
        ),
    )(info, w_query, w_key, w_value)


def halves_body_prefetch(chunks, info, *refs):
    halves_body(chunks, *refs)


def adjoint_body(parts, info, ids, sensors, *refs):
    outs, rows = refs[:parts], refs[parts]
    count = sensors.shape[0]
    columns = outs[0].shape[1]
    local = ids[...] - info[2] * count
    chosen = lax.broadcasted_iota(jnp.int32, (count, count), 0) == local
    rows[...] = dot(chosen.astype(F32), sensors[...], NN)
    for r in range(parts):
        start = pl.multiple_of((info[2] ^ r) * columns, LANES)
        outs[r][...] = rows[:, pl.ds(start, columns)]


def stack_body(parts, *refs):
    rows = refs[0].shape[0]
    for r in range(parts):
        refs[parts][r * rows : (r + 1) * rows, :] = refs[r][...]


def attention_body(chunk, blocks, pieces, info, neighbours, *refs):
    x, wq, wk, wv = refs[:4]
    halves = refs[4 : 4 + len(pieces)]
    adjoints = refs[4 + len(pieces) : 4 + len(pieces) + blocks]
    out, panel, proj = refs[4 + len(pieces) + blocks :]
    z, y, t = info[0], info[1], info[2]
    cols = slice(chunk * LANES, (chunk + 1) * LANES)
    own = wq.shape[0]
    rows = pl.ds(pl.multiple_of(z * own, 8), own)
    panel[rows, 0:LANES] = wq[:, cols]
    panel[rows, LANES : 2 * LANES] = wk[:, cols]
    panel[rows, 2 * LANES : 3 * LANES] = wv[:, cols]
    for (r, g), half in zip(pieces, halves):
        count = half.shape[0]
        start = (z ^ r) * own + (y ^ g) * count
        panel[pl.ds(pl.multiple_of(start, 8), count), :] = half[...]
    attention_core(cols, blocks, t, neighbours, x, panel, adjoints, out, proj)


def attention_panel_body(chunk, blocks, info, neighbours, x, panel, *refs):
    cols = slice(chunk * LANES, (chunk + 1) * LANES)
    attention_core(
        cols, blocks, info[2], neighbours, x, panel, refs[:blocks], refs[blocks], refs[blocks + 1]
    )


def attention_core(cols, blocks, t, neighbours, x, panel, adjoints, out, proj):
    proj[...] = dot(x[...], panel[...], NN)
    out[:, LANES:] = jnp.zeros((out.shape[0], 2 * LANES), F32)
    first = lax.broadcasted_iota(jnp.int32, (BLOCK, LANES), 1) < DH
    scale = DH ** (-0.5)

    def by_head(value):
        return jnp.concatenate(
            [jnp.where(first, value, 0.0), jnp.where(first, 0.0, value)], axis=0
        )

    for r in range(blocks):
        here = slice(r * BLOCK, (r + 1) * BLOCK)
        there = [
            pl.ds(pl.multiple_of((neighbours[t ^ r, j] ^ t) * BLOCK, BLOCK), BLOCK)
            for j in range(KB)
        ]
        query = by_head(proj[here, 0:LANES])
        adjoint = by_head(adjoints[r][:, cols])
        key = jnp.concatenate([proj[w, LANES : 2 * LANES] for w in there], axis=0)
        value = jnp.concatenate([proj[w, 2 * LANES :] for w in there], axis=0)
        scores = dot(query, key, NT) * scale
        raised = jnp.exp(scores - jnp.max(scores, axis=1, keepdims=True))
        attention = raised / jnp.sum(raised, axis=1, keepdims=True)
        weight_adjoint = dot(adjoint, value, NT)
        row_dots = jnp.sum(attention * weight_adjoint, axis=1, keepdims=True)
        score_adjoint = attention * (weight_adjoint - row_dots) * scale
        both = dot(score_adjoint, key, NN)
        out[here, 0:LANES] = jnp.where(first, both[:BLOCK], both[BLOCK:])
        dkey = dot(score_adjoint, query, TN)
        dvalue = dot(attention, adjoint, TN)
        for j, w in enumerate(there):
            part = slice(j * BLOCK, (j + 1) * BLOCK)
            out[w, LANES : 2 * LANES] += dkey[part]
            out[w, 2 * LANES :] += dvalue[part]


def weight_grad_body(shares, rows, info, x, stacked, out):
    for j, r in enumerate(shares):
        start = pl.multiple_of((info[0] ^ r) * rows, LANES)
        out[j * rows : (j + 1) * rows, :] = dot(x[:, pl.ds(start, rows)], stacked[...], TN)


def whole_grad_body(x, stacked, out):
    out[...] = dot(x[...], stacked[...], TN)


def back_body(shares, chunks, *refs):
    stacked, panels, out = refs[:chunks], refs[chunks : 2 * chunks], refs[2 * chunks]
    total = None
    for c in range(chunks):
        rows = jnp.concatenate(
            [stacked[c][r * BLOCK : (r + 1) * BLOCK, :] for r in shares], axis=0
        )
        term = dot(rows, panels[c][...], NT)
        total = term if total is None else total + term
    out[...] = total


def scatter_halving(send, keep, axis, size, rows):
    step = 1
    while True:
        got = swap(send, axis, size, step)
        step *= 2
        if step == size:
            return keep, got
        total = (keep + got).reshape(-1, 2, rows, keep.shape[1])
        send, keep = total[:, 1].reshape(-1, keep.shape[1]), total[:, 0].reshape(-1, keep.shape[1])


def per_device(sizes, node_features, sensor_adjoint, sensor_node, neighbours, *weights):
    grp, wa, ta = sizes
    hour_rows = node_features[0]
    nodes_here, width = hour_rows.shape
    rows_here, columns = weights[0].shape
    chunks = columns // LANES
    blocks = ta
    nodes = nodes_here * ta
    z, y, t = lax.axis_index("wa"), lax.axis_index("grp"), lax.axis_index("ta")
    info = jnp.stack([z, y, t]).astype(jnp.int32)
    direct = rows_here % LANES == 0 and rows_here % (8 * grp) == 0 and wa > 1

    held = {0: hour_rows}
    step = ta
    while step > 1:
        step //= 2
        held.update({r | step: swap(v, "ta", ta, step) for r, v in list(held.items())})
    inputs = local_call(
        functools.partial(stack_body, ta), [shaped(nodes, width)], [held[r] for r in range(ta)]
    )[0]

    blocks_out = local_call(
        functools.partial(adjoint_body, ta),
        [shaped(nodes_here, columns)] * ta,
        [sensor_node.reshape(1, -1), sensor_adjoint[0]],
        scalars=[info],
        scratch=[pltpu.VMEM((nodes_here, width), F32)],
        flops=12 * nodes_here * nodes_here * width,
    )
    adjoints = [blocks_out[0]] + [swap(blocks_out[r], "ta", ta, r) for r in range(1, ta)]

    stacked, panels, owned = [], [], []
    if direct:
        half = rows_here // grp
        halves = weight_halves(info, *weights, half, chunks)
    for c in range(chunks):
        proj_flops = 12 * nodes * width * 3 * LANES + 60 * 2 * nodes * 4 * BLOCK * LANES
        scratch = [pltpu.VMEM((nodes, 3 * LANES), F32)]
        if direct:
            mine = {0: halves[c]}
            step = wa
            while step > 1:
                step //= 2
                mine.update({r | step: swap(v, "wa", wa, step) for r, v in list(mine.items())})
            pieces = {(r, 0): mine[r] for r in range(1, wa)}
            for g in range(1, grp):
                pieces.update({(r, g): swap(mine[r], "grp", grp, g) for r in range(1, wa)})
            names = sorted(pieces)
            dqkv, panel = local_call(
                functools.partial(attention_body, c, blocks, names),
                [shaped(nodes, 3 * LANES), shaped(width, 3 * LANES)],
                [inputs, *weights, *[pieces[n] for n in names], *adjoints],
                scalars=[info, neighbours],
                scratch=scratch,
                flops=proj_flops,
            )
        else:
            cols = slice(c * LANES, (c + 1) * LANES)
            local = jnp.concatenate([w[:, cols] for w in weights], axis=1)
            panel = lax.all_gather(local, "wa", axis=0, tiled=True)
            dqkv = local_call(
                functools.partial(attention_panel_body, c, blocks),
                [shaped(nodes, 3 * LANES)],
                [inputs, panel, *adjoints],
                scalars=[info, neighbours],
                scratch=scratch,
                flops=proj_flops,
            )[0]
        stacked.append(dqkv)
        panels.append(panel)
        if direct:
            sends = [
                local_call(
                    functools.partial(weight_grad_body, range(odd, wa, 2), rows_here),
                    [shaped(rows_here * wa // 2, 3 * LANES)],
                    [inputs, dqkv],
                    scalars=[info],
                    flops=12 * nodes * rows_here * wa // 2 * 3 * LANES,
                )[0]
                for odd in (1, 0)
            ]
            kept, got = scatter_halving(*sends, "wa", wa, rows_here)
            owned.append(kept + got)
        else:
            full = local_call(
                whole_grad_body,
                [shaped(width, 3 * LANES)],
                [inputs, dqkv],
                flops=12 * nodes * width * 3 * LANES,
            )[0]
            owned.append(lax.psum_scatter(full, "wa", scatter_dimension=0, tiled=True))

    backs = [
        local_call(
            functools.partial(back_body, range(odd, ta, 2), chunks),
            [shaped(nodes // 2, width)],
            [*stacked, *panels],
            flops=12 * nodes // 2 * width * columns * 3,
        )[0]
        for odd in (1, 0)
    ]
    kept, got = scatter_halving(*backs, "ta", ta, nodes_here)
    grads = [
        jnp.concatenate([o[:, i * LANES : (i + 1) * LANES] for o in owned], axis=1)
        for i in range(3)
    ]
    return ((kept + got)[None], *grads)


def solution(mesh):
    sizes = tuple(mesh.shape[name] for name in ("grp", "wa", "ta"))
    return jax.shard_map(
        functools.partial(per_device, sizes),
        mesh=mesh,
        in_specs=(
            P(("grp", "wa"), "ta", None),
            P(("grp", "wa"), "ta", None),
            P("ta"),
            P(),
            P("wa", "ta"),
            P("wa", "ta"),
            P("wa", "ta"),
        ),
        out_specs=(
            P(("grp", "wa"), "ta", None),
            P(("grp", "wa"), "ta"),
            P(("grp", "wa"), "ta"),
            P(("grp", "wa"), "ta"),
        ),
        check_vma=False,
    )
```

```python
import functools

import jax
import jax.numpy as jnp
from jax import lax
from jax.experimental import pallas as pl
from jax.experimental.pallas import tpu as pltpu
from jax.sharding import PartitionSpec as P

DH = 64
BLOCK = 128
KB = 2
LANES = 128
F32 = jnp.float32
NN = ((1,), (0,))
NT = ((1,), (1,))
TN = ((0,), (0,))


def dot(left, right, dims):
    return lax.dot_general(
        left, right, (dims, ((), ())), precision=lax.Precision.HIGHEST, preferred_element_type=F32
    )


def local_call(body, outs, args, scalars=(), scratch=(), flops=0, vmem_mib=24):
    vmem = pl.BlockSpec(memory_space=pltpu.VMEM)
    smem = pl.BlockSpec(memory_space=pltpu.SMEM)
    return pl.pallas_call(
        body,
        out_shape=outs,
        in_specs=[smem] * len(scalars) + [vmem] * len(args),
        out_specs=[vmem] * len(outs),
        scratch_shapes=scratch,
        cost_estimate=pl.CostEstimate(flops=flops, bytes_accessed=flops // 256, transcendentals=0),
        compiler_params=pltpu.CompilerParams(vmem_limit_bytes=vmem_mib << 20),
    )(*scalars, *args)


def shaped(*shape):
    return jax.ShapeDtypeStruct(shape, F32)


def swap(value, axis, size, step):
    return lax.ppermute(value, axis, [(i, i ^ step) for i in range(size)])


def after(value, *others):
    return lax.optimization_barrier((value, *others))[0]


def halves_body(chunks, wq, wk, wv, *outs):
    for c in range(chunks):
        cols = slice(c * LANES, (c + 1) * LANES)
        outs[c][:, 0:LANES] = wq[:, cols]
        outs[c][:, LANES : 2 * LANES] = wk[:, cols]
        outs[c][:, 2 * LANES : 3 * LANES] = wv[:, cols]


def weight_halves(info, w_query, w_key, w_value, rows, chunks):
    columns = w_query.shape[1]
    spec = pl.BlockSpec((rows, columns), lambda i, info: (info[1], 0))
    out = pl.BlockSpec((rows, 3 * LANES), lambda i, info: (0, 0))
    return pl.pallas_call(
        functools.partial(halves_body_prefetch, chunks),
        out_shape=[shaped(rows, 3 * LANES)] * chunks,
        grid_spec=pltpu.PrefetchScalarGridSpec(
            num_scalar_prefetch=1, grid=(1,), in_specs=[spec] * 3, out_specs=[out] * chunks
        ),
    )(info, w_query, w_key, w_value)


def halves_body_prefetch(chunks, info, *refs):
    halves_body(chunks, *refs)


def adjoint_body(parts, info, ids, sensors, *refs):
    outs, rows = refs[:parts], refs[parts]
    count = sensors.shape[0]
    columns = outs[0].shape[1]
    local = ids[...] - info[2] * count
    chosen = lax.broadcasted_iota(jnp.int32, (count, count), 0) == local
    rows[...] = dot(chosen.astype(F32), sensors[...], NN)
    for r in range(parts):
        start = pl.multiple_of((info[2] ^ r) * columns, LANES)
        outs[r][...] = rows[:, pl.ds(start, columns)]


def stack_body(parts, *refs):
    rows = refs[0].shape[0]
    for r in range(parts):
        refs[parts][r * rows : (r + 1) * rows, :] = refs[r][...]


def attention_body(chunk, blocks, pieces, info, neighbours, *refs):
    x, wq, wk, wv = refs[:4]
    halves = refs[4 : 4 + len(pieces)]
    adjoints = refs[4 + len(pieces) : 4 + len(pieces) + blocks]
    out, panel, proj = refs[4 + len(pieces) + blocks :]
    z, y, t = info[0], info[1], info[2]
    cols = slice(chunk * LANES, (chunk + 1) * LANES)
    own = wq.shape[0]
    rows = pl.ds(pl.multiple_of(z * own, 8), own)
    panel[rows, 0:LANES] = wq[:, cols]
    panel[rows, LANES : 2 * LANES] = wk[:, cols]
    panel[rows, 2 * LANES : 3 * LANES] = wv[:, cols]
    for (r, g), half in zip(pieces, halves):
        count = half.shape[0]
        start = (z ^ r) * own + (y ^ g) * count
        panel[pl.ds(pl.multiple_of(start, 8), count), :] = half[...]
    attention_core(cols, blocks, t, neighbours, x, panel, adjoints, out, proj)


def attention_panel_body(chunk, blocks, info, neighbours, x, panel, *refs):
    cols = slice(chunk * LANES, (chunk + 1) * LANES)
    attention_core(
        cols, blocks, info[2], neighbours, x, panel, refs[:blocks], refs[blocks], refs[blocks + 1]
    )


def attention_core(cols, blocks, t, neighbours, x, panel, adjoints, out, proj):
    proj[...] = dot(x[...], panel[...], NN)
    out[:, LANES:] = jnp.zeros((out.shape[0], 2 * LANES), F32)
    first = lax.broadcasted_iota(jnp.int32, (BLOCK, LANES), 1) < DH
    scale = DH ** (-0.5)

    def by_head(value):
        return jnp.concatenate(
            [jnp.where(first, value, 0.0), jnp.where(first, 0.0, value)], axis=0
        )

    for r in range(blocks):
        here = slice(r * BLOCK, (r + 1) * BLOCK)
        there = [
            pl.ds(pl.multiple_of((neighbours[t ^ r, j] ^ t) * BLOCK, BLOCK), BLOCK)
            for j in range(KB)
        ]
        query = by_head(proj[here, 0:LANES])
        adjoint = by_head(adjoints[r][:, cols])
        key = jnp.concatenate([proj[w, LANES : 2 * LANES] for w in there], axis=0)
        value = jnp.concatenate([proj[w, 2 * LANES :] for w in there], axis=0)
        scores = dot(query, key, NT) * scale
        raised = jnp.exp(scores - jnp.max(scores, axis=1, keepdims=True))
        attention = raised / jnp.sum(raised, axis=1, keepdims=True)
        weight_adjoint = dot(adjoint, value, NT)
        row_dots = jnp.sum(attention * weight_adjoint, axis=1, keepdims=True)
        score_adjoint = attention * (weight_adjoint - row_dots) * scale
        both = dot(score_adjoint, key, NN)
        out[here, 0:LANES] = jnp.where(first, both[:BLOCK], both[BLOCK:])
        dkey = dot(score_adjoint, query, TN)
        dvalue = dot(attention, adjoint, TN)
        for j, w in enumerate(there):
            part = slice(j * BLOCK, (j + 1) * BLOCK)
            out[w, LANES : 2 * LANES] += dkey[part]
            out[w, 2 * LANES :] += dvalue[part]


def weight_grad_body(shares, rows, info, x, stacked, out):
    for j, r in enumerate(shares):
        start = pl.multiple_of((info[0] ^ r) * rows, LANES)
        out[j * rows : (j + 1) * rows, :] = dot(x[:, pl.ds(start, rows)], stacked[...], TN)


def whole_grad_body(x, stacked, out):
    out[...] = dot(x[...], stacked[...], TN)


def back_body(shares, chunks, *refs):
    stacked, panels, out = refs[:chunks], refs[chunks : 2 * chunks], refs[2 * chunks]
    total = None
    for c in range(chunks):
        rows = jnp.concatenate(
            [stacked[c][r * BLOCK : (r + 1) * BLOCK, :] for r in shares], axis=0
        )
        term = dot(rows, panels[c][...], NT)
        total = term if total is None else total + term
    out[...] = total


def halve_body(rows, keep, got, send, kept):
    for j in range(keep.shape[0] // rows):
        out = send if j % 2 else kept
        place = slice(j // 2 * rows, (j // 2 + 1) * rows)
        here = slice(j * rows, (j + 1) * rows)
        out[place, :] = keep[here, :] + got[here, :]


def scatter_halving(send, keep, axis, size, rows, wait=()):
    step, first = 1, None
    while True:
        got = swap(send, axis, size, step)
        step *= 2
        if step == size:
            return keep, got, first
        got = after(got, *wait) if wait else got
        shape = shaped(keep.shape[0] // 2, keep.shape[1])
        send, keep = local_call(functools.partial(halve_body, rows), [shape] * 2, [keep, got])
        first = keep if first is None else first


def join_body(chunks, *refs):
    for c in range(chunks):
        for i in range(3):
            part = slice(i * LANES, (i + 1) * LANES)
            term = refs[2 * c][:, part] + refs[2 * c + 1][:, part]
            refs[2 * chunks + i][:, c * LANES : (c + 1) * LANES] = term


def per_device(sizes, node_features, sensor_adjoint, sensor_node, neighbours, *weights):
    grp, wa, ta = sizes
    hour_rows = node_features[0]
    nodes_here, width = hour_rows.shape
    rows_here, columns = weights[0].shape
    chunks = columns // LANES
    blocks = ta
    nodes = nodes_here * ta
    z, y, t = lax.axis_index("wa"), lax.axis_index("grp"), lax.axis_index("ta")
    info = jnp.stack([z, y, t]).astype(jnp.int32)
    direct = rows_here % LANES == 0 and rows_here % (8 * grp) == 0 and wa > 1

    first = []
    if direct:
        half = rows_here // grp
        halves = weight_halves(info, *weights, half, chunks)
        gathered, crossed, last = [], [], None
        for c in range(chunks):
            mine = {0: halves[c] if last is None else after(halves[c], last)}
            step = wa
            while step > 1:
                step //= 2
                mine.update({r | step: swap(v, "wa", wa, step) for r, v in list(mine.items())})
            last = mine[wa // 2]
            gathered.append(mine)
            crossed.append(
                {(r, g): swap(mine[r], "grp", grp, g) for g in range(1, grp) for r in range(1, wa)}
            )

        first = [gathered[0][1]]

    held = {0: hour_rows}
    step = ta
    while step > 1:
        step //= 2
        held.update(
            {
                r | step: swap(after(v, *first) if r else v, "ta", ta, step)
                for r, v in list(held.items())
            }
        )
    inputs = local_call(
        functools.partial(stack_body, ta), [shaped(nodes, width)], [held[r] for r in range(ta)]
    )[0]

    blocks_out = local_call(
        functools.partial(adjoint_body, ta),
        [shaped(nodes_here, columns)] * ta,
        [sensor_node.reshape(1, -1), sensor_adjoint[0]],
        scalars=[info],
        scratch=[pltpu.VMEM((nodes_here, width), F32)],
        flops=12 * nodes_here * nodes_here * width,
    )
    adjoints = [blocks_out[0]] + [
        swap(after(blocks_out[r], held[ta // 2]), "ta", ta, r) for r in range(1, ta)
    ]

    stacked, panels, owned, firsts = [], [], [], []
    for c in range(chunks):
        turn = after(info, stacked[-1]) if stacked else info
        more = direct and c + 1 < chunks
        if more:
            turn = after(turn, *[gathered[c + 1][r] for r in range(1, wa)])
        proj_flops = 12 * nodes * width * 3 * LANES + 60 * 2 * nodes * 4 * BLOCK * LANES
        scratch = [pltpu.VMEM((nodes, 3 * LANES), F32)]
        if direct:
            pieces = {(r, 0): gathered[c][r] for r in range(1, wa)}
            pieces.update(crossed[c])
            names = sorted(pieces)
            dqkv, panel = local_call(
                functools.partial(attention_body, c, blocks, names),
                [shaped(nodes, 3 * LANES), shaped(width, 3 * LANES)],
                [inputs, *weights, *[pieces[n] for n in names], *adjoints],
                scalars=[turn, neighbours],
                scratch=scratch,
                flops=proj_flops,
            )
        else:
            cols = slice(c * LANES, (c + 1) * LANES)
            local = jnp.concatenate([w[:, cols] for w in weights], axis=1)
            panel = lax.all_gather(local, "wa", axis=0, tiled=True)
            dqkv = local_call(
                functools.partial(attention_panel_body, c, blocks),
                [shaped(nodes, 3 * LANES)],
                [inputs, panel, *adjoints],
                scalars=[turn, neighbours],
                scratch=scratch,
                flops=proj_flops,
            )[0]
        stacked.append(dqkv)
        panels.append(panel)
        if direct:
            later = after(info, dqkv, *crossed[c + 1].values()) if more else info
            sends = [
                local_call(
                    functools.partial(weight_grad_body, range(odd, wa, 2), rows_here),
                    [shaped(rows_here * wa // 2, 3 * LANES)],
                    [inputs, dqkv],
                    scalars=[later],
                )[0]
                for odd in (1, 0)
            ]
            kept, got, early = scatter_halving(*sends, "wa", wa, rows_here, owned[-1:])
            owned += [kept, got]
            firsts = (firsts or [early]) if more else [*firsts, sends[0]]
        else:
            full = local_call(
                whole_grad_body,
                [shaped(width, 3 * LANES)],
                [inputs, dqkv],
                flops=12 * nodes * width * 3 * LANES,
            )[0]
            owned.append(lax.psum_scatter(full, "wa", scatter_dimension=0, tiled=True))

    backs = [
        local_call(
            functools.partial(back_body, range(odd, ta, 2), chunks),
            [shaped(nodes // 2, width)],
            [*stacked, *[after(p, *firsts) for p in panels]],
        )[0]
        for odd in (1, 0)
    ]
    kept, got, _ = scatter_halving(*backs, "ta", ta, nodes_here)
    if direct:
        grads = local_call(
            functools.partial(join_body, chunks), [shaped(rows_here, columns)] * 3, owned
        )
    else:
        grads = [
            jnp.concatenate([o[:, i * LANES : (i + 1) * LANES] for o in owned], axis=1)
            for i in range(3)
        ]
    return ((kept + got)[None], *grads)


def solution(mesh):
    sizes = tuple(mesh.shape[name] for name in ("grp", "wa", "ta"))
    return jax.shard_map(
        functools.partial(per_device, sizes),
        mesh=mesh,
        in_specs=(
            P(("grp", "wa"), "ta", None),
            P(("grp", "wa"), "ta", None),
            P("ta"),
            P(),
            P("wa", "ta"),
            P("wa", "ta"),
            P("wa", "ta"),
        ),
        out_specs=(
            P(("grp", "wa"), "ta", None),
            P(("grp", "wa"), "ta"),
            P(("grp", "wa"), "ta"),
            P(("grp", "wa"), "ta"),
        ),
        check_vma=False,
    )
```

```python
import functools

import jax
import jax.numpy as jnp
from jax import lax
from jax.experimental import pallas as pl
from jax.experimental.pallas import tpu as pltpu
from jax.sharding import PartitionSpec as P

DH = 64
BLOCK = 128
KB = 2
LANES = 128
F32 = jnp.float32
NN = ((1,), (0,))
NT = ((1,), (1,))
TN = ((0,), (0,))


def dot(left, right, dims):
    return lax.dot_general(
        left, right, (dims, ((), ())), precision=lax.Precision.HIGHEST, preferred_element_type=F32
    )


def local_call(body, outs, args, scalars=(), scratch=(), flops=0, vmem_mib=24):
    vmem = pl.BlockSpec(memory_space=pltpu.VMEM)
    smem = pl.BlockSpec(memory_space=pltpu.SMEM)
    return pl.pallas_call(
        body,
        out_shape=outs,
        in_specs=[smem] * len(scalars) + [vmem] * len(args),
        out_specs=[vmem] * len(outs),
        scratch_shapes=scratch,
        cost_estimate=pl.CostEstimate(flops=flops, bytes_accessed=flops // 256, transcendentals=0),
        compiler_params=pltpu.CompilerParams(vmem_limit_bytes=vmem_mib << 20),
    )(*scalars, *args)


def shaped(*shape):
    return jax.ShapeDtypeStruct(shape, F32)


def swap(value, axis, size, step):
    return lax.ppermute(value, axis, [(i, i ^ step) for i in range(size)])


def after(value, *others):
    return lax.optimization_barrier((value, *others))[0]


def entry_body(parts, info, ids, sensors, wq, wk, wv, packed, *refs):
    if packed is not None:
        packed[:, 0:LANES] = wq[...]
        packed[:, LANES : 2 * LANES] = wk[...]
        packed[:, 2 * LANES :] = wv[...]
    outs, rows = refs[:parts], refs[parts]
    count = sensors.shape[0]
    columns = outs[0].shape[1]
    local = ids[...] - info[2] * count
    chosen = lax.broadcasted_iota(jnp.int32, (count, count), 0) == local
    rows[...] = dot(chosen.astype(F32), sensors[...], NN)
    for r in range(parts):
        start = pl.multiple_of((info[2] ^ r) * columns, LANES)
        outs[r][...] = rows[:, pl.ds(start, columns)]


def entry(info, ids, sensors, weights, parts, direct):
    rows, columns = weights[0].shape
    count, width = sensors.shape

    def whole(*shape):
        return pl.BlockSpec(shape, lambda i, info: (0, 0))

    spec = pl.BlockSpec((rows, LANES), lambda i, info: (0, info[1]))
    body = entry_body if direct else adjoint_body
    outs = ([(rows, 3 * LANES)] if direct else []) + [(count, columns)] * parts
    return pl.pallas_call(
        functools.partial(body, parts),
        out_shape=[shaped(*o) for o in outs],
        grid_spec=pltpu.PrefetchScalarGridSpec(
            num_scalar_prefetch=1,
            grid=(1,),
            in_specs=[whole(1, count), whole(count, width)] + ([spec] * 3 if direct else []),
            out_specs=[whole(*o) for o in outs],
            scratch_shapes=[pltpu.VMEM((count, width), F32)],
        ),
        compiler_params=pltpu.CompilerParams(vmem_limit_bytes=60 << 20),
    )(info, ids, sensors, *(weights if direct else ()))


def columns_of(turn, info):
    return pl.ds(pl.multiple_of((info[1] ^ turn) * LANES, LANES), LANES)


def spread(held, axis, size):
    held, step = dict(held), size
    while step > 1:
        step //= 2
        if step not in held:
            held.update({r | step: swap(v, axis, size, step) for r, v in list(held.items())})
    return held


def adjoint_body(parts, info, ids, sensors, *refs):
    entry_body(parts, info, ids, sensors, None, None, None, None, *refs)


def stack_body(parts, *refs):
    rows = refs[0].shape[0]
    for r in range(parts):
        refs[parts][r * rows : (r + 1) * rows, :] = refs[r][...]


def attention_body(turn, blocks, wa, info, neighbours, *refs):
    x, wq, wk, wv = refs[:4]
    pieces = refs[4 : 3 + wa]
    adjoints = refs[3 + wa : 3 + wa + blocks]
    out, panel, proj = refs[3 + wa + blocks :]
    cols = columns_of(turn, info)
    count = wq.shape[0]

    def rows(r):
        return pl.ds(pl.multiple_of((info[0] ^ r) * count, 8), count)

    panel[rows(0), 0:LANES] = wq[:, cols]
    panel[rows(0), LANES : 2 * LANES] = wk[:, cols]
    panel[rows(0), 2 * LANES : 3 * LANES] = wv[:, cols]
    for r in range(1, wa):
        panel[rows(r), :] = pieces[r - 1][...]
    attention_core(cols, blocks, info[2], neighbours, x, panel, adjoints, out, proj)


def attention_panel_body(chunk, blocks, info, neighbours, x, panel, *refs):
    cols = slice(chunk * LANES, (chunk + 1) * LANES)
    attention_core(
        cols, blocks, info[2], neighbours, x, panel, refs[:blocks], refs[blocks], refs[blocks + 1]
    )


def attention_core(cols, blocks, t, neighbours, x, panel, adjoints, out, proj):
    proj[...] = dot(x[...], panel[...], NN)
    out[:, LANES:] = jnp.zeros((out.shape[0], 2 * LANES), F32)
    first = lax.broadcasted_iota(jnp.int32, (BLOCK, LANES), 1) < DH
    scale = DH ** (-0.5)

    def by_head(value):
        return jnp.concatenate(
            [jnp.where(first, value, 0.0), jnp.where(first, 0.0, value)], axis=0
        )

    for r in range(blocks):
        here = slice(r * BLOCK, (r + 1) * BLOCK)
        there = [
            pl.ds(pl.multiple_of((neighbours[t ^ r, j] ^ t) * BLOCK, BLOCK), BLOCK)
            for j in range(KB)
        ]
        query = by_head(proj[here, 0:LANES])
        adjoint = by_head(adjoints[r][:, cols])
        key = jnp.concatenate([proj[w, LANES : 2 * LANES] for w in there], axis=0)
        value = jnp.concatenate([proj[w, 2 * LANES :] for w in there], axis=0)
        scores = dot(query, key, NT) * scale
        raised = jnp.exp(scores - jnp.max(scores, axis=1, keepdims=True))
        attention = raised / jnp.sum(raised, axis=1, keepdims=True)
        weight_adjoint = dot(adjoint, value, NT)
        row_dots = jnp.sum(attention * weight_adjoint, axis=1, keepdims=True)
        score_adjoint = attention * (weight_adjoint - row_dots) * scale
        both = dot(score_adjoint, key, NN)
        out[here, 0:LANES] = jnp.where(first, both[:BLOCK], both[BLOCK:])
        dkey = dot(score_adjoint, query, TN)
        dvalue = dot(attention, adjoint, TN)
        for j, w in enumerate(there):
            part = slice(j * BLOCK, (j + 1) * BLOCK)
            out[w, LANES : 2 * LANES] += dkey[part]
            out[w, 2 * LANES :] += dvalue[part]


def weight_grad_body(shares, rows, info, x, stacked, out):
    for j, r in enumerate(shares):
        start = pl.multiple_of((info[0] ^ r) * rows, LANES)
        out[j * rows : (j + 1) * rows, :] = dot(x[:, pl.ds(start, rows)], stacked[...], TN)


def whole_grad_body(x, stacked, out):
    out[...] = dot(x[...], stacked[...], TN)


def back_body(shares, chunks, *refs):
    stacked, panels, out = refs[:chunks], refs[chunks : 2 * chunks], refs[2 * chunks]
    total = None
    for c in range(chunks):
        rows = jnp.concatenate(
            [stacked[c][r * BLOCK : (r + 1) * BLOCK, :] for r in shares], axis=0
        )
        term = dot(rows, panels[c][...], NT)
        total = term if total is None else total + term
    out[...] = total


def halve_body(rows, keep, got, send, kept):
    for j in range(keep.shape[0] // rows):
        out = send if j % 2 else kept
        place = slice(j // 2 * rows, (j // 2 + 1) * rows)
        here = slice(j * rows, (j + 1) * rows)
        out[place, :] = keep[here, :] + got[here, :]


def scatter_halving(send, keep, axis, size, rows, wait=()):
    step, first = 1, None
    while True:
        got = swap(send, axis, size, step)
        step *= 2
        if step == size:
            return keep, got, first
        got = after(got, *wait) if wait else got
        shape = shaped(keep.shape[0] // 2, keep.shape[1])
        send, keep = local_call(functools.partial(halve_body, rows), [shape] * 2, [keep, got])
        first = keep if first is None else first


def join_body(turns, info, *refs):
    for turn in range(turns):
        for i in range(3):
            part = slice(i * LANES, (i + 1) * LANES)
            term = refs[2 * turn][:, part] + refs[2 * turn + 1][:, part]
            refs[2 * turns + i][:, columns_of(turn, info)] = term


def per_device(sizes, node_features, sensor_adjoint, sensor_node, neighbours, *weights):
    grp, wa, ta = sizes
    hour_rows = node_features[0]
    nodes_here, width = hour_rows.shape
    rows_here, columns = weights[0].shape
    chunks = columns // LANES
    blocks = ta
    nodes = nodes_here * ta
    z, y, t = lax.axis_index("wa"), lax.axis_index("grp"), lax.axis_index("ta")
    info = jnp.stack([z, y, t]).astype(jnp.int32)
    direct = rows_here % LANES == 0 and chunks == grp == 2 and wa > 1

    blocks_out = entry(info, sensor_node.reshape(1, -1), sensor_adjoint[0], weights, ta, direct)
    held = {0: hour_rows}
    if direct:
        first, *blocks_out = blocks_out
        held[0] = after(hour_rows, first)
        gathered = [spread({0: first}, "wa", wa)]
        gathered.append({r: swap(gathered[0][r], "grp", grp, 1) for r in range(1, wa)})
        held[ta // 2] = after(swap(held[0], "ta", ta, ta // 2), gathered[0][1])
    held = spread(held, "ta", ta)
    adjoints = [blocks_out[0]] + [
        swap(after(blocks_out[r], held[ta // 2]), "ta", ta, r) for r in range(1, ta)
    ]
    inputs = local_call(
        functools.partial(stack_body, ta), [shaped(nodes, width)], [held[r] for r in range(ta)]
    )[0]

    stacked, panels, owned, firsts = [], [], [], []
    for c in range(chunks):
        proj_flops = 12 * nodes * width * 3 * LANES + 60 * 2 * nodes * 4 * BLOCK * LANES
        scratch = [pltpu.VMEM((nodes, 3 * LANES), F32)]
        turn = after(info, stacked[-1]) if stacked else info
        if direct:
            dqkv, panel = local_call(
                functools.partial(attention_body, c, blocks, wa),
                [shaped(nodes, 3 * LANES), shaped(width, 3 * LANES)],
                [inputs, *weights, *[gathered[c][r] for r in range(1, wa)], *adjoints],
                scalars=[turn, neighbours],
                scratch=scratch,
                flops=proj_flops,
            )
            later = info if c else after(info, dqkv, *[gathered[1][r] for r in range(1, wa - 1)])
            sends = [
                local_call(
                    functools.partial(weight_grad_body, range(odd, wa, 2), rows_here),
                    [shaped(rows_here * wa // 2, 3 * LANES)],
                    [inputs, dqkv],
                    scalars=[later],
                )[0]
                for odd in (1, 0)
            ]
            kept, got, early = scatter_halving(*sends, "wa", wa, rows_here, owned[-1:])
            owned += [kept, got]
            firsts += [sends[0]] if c else [early]
        else:
            cols = slice(c * LANES, (c + 1) * LANES)
            local = jnp.concatenate([w[:, cols] for w in weights], axis=1)
            panel = lax.all_gather(local, "wa", axis=0, tiled=True)
            dqkv = local_call(
                functools.partial(attention_panel_body, c, blocks),
                [shaped(nodes, 3 * LANES)],
                [inputs, panel, *adjoints],
                scalars=[turn, neighbours],
                scratch=scratch,
                flops=proj_flops,
            )[0]
            full = local_call(whole_grad_body, [shaped(width, 3 * LANES)], [inputs, dqkv])[0]
            owned.append(lax.psum_scatter(full, "wa", scatter_dimension=0, tiled=True))
        stacked.append(dqkv)
        panels.append(panel)

    backs = [
        local_call(
            functools.partial(back_body, range(odd, ta, 2), chunks),
            [shaped(nodes // 2, width)],
            [*stacked, *[after(p, *firsts) for p in panels]],
        )[0]
        for odd in (1, 0)
    ]
    kept, got, _ = scatter_halving(*backs, "ta", ta, nodes_here)
    back = (kept + got)[None]
    if direct:
        owned[-1] = after(owned[-1], back)
        grads = local_call(
            functools.partial(join_body, chunks),
            [shaped(rows_here, columns)] * 3,
            owned,
            scalars=[info],
        )
    else:
        grads = [
            jnp.concatenate([o[:, i * LANES : (i + 1) * LANES] for o in owned], axis=1)
            for i in range(3)
        ]
    return (back, *grads)


def solution(mesh):
    sizes = tuple(mesh.shape[name] for name in ("grp", "wa", "ta"))
    return jax.shard_map(
        functools.partial(per_device, sizes),
        mesh=mesh,
        in_specs=(
            P(("grp", "wa"), "ta", None),
            P(("grp", "wa"), "ta", None),
            P("ta"),
            P(),
            P("wa", "ta"),
            P("wa", "ta"),
            P("wa", "ta"),
        ),
        out_specs=(
            P(("grp", "wa"), "ta", None),
            P(("grp", "wa"), "ta"),
            P(("grp", "wa"), "ta"),
            P(("grp", "wa"), "ta"),
        ),
        check_vma=False,
    )
```

```python
import functools

import jax
import jax.numpy as jnp
from jax import lax
from jax.experimental import pallas as pl
from jax.experimental.pallas import tpu as pltpu
from jax.sharding import PartitionSpec as P

DH = 64
BLOCK = 128
KB = 2
GATE = (1,)
LANES = 128
F32 = jnp.float32
NN = ((1,), (0,))
NT = ((1,), (1,))
TN = ((0,), (0,))


def dot(left, right, dims):
    return lax.dot_general(
        left, right, (dims, ((), ())), precision=lax.Precision.HIGHEST, preferred_element_type=F32
    )


def grads_of(shares, info, inputs, stacked, rows):
    return local_call(
        functools.partial(weight_grad_body, shares, rows),
        [shaped(rows * len(shares), stacked.shape[1])],
        [inputs, stacked],
        scalars=[info],
    )[0]


def total_of(kept, got, rows):
    return local_call(
        functools.partial(sum_body, rows), [shaped(rows, kept.shape[1])], [kept, got]
    )[0]


def local_call(body, outs, args, scalars=(), scratch=(), flops=0, vmem_mib=24):
    vmem = pl.BlockSpec(memory_space=pltpu.VMEM)
    smem = pl.BlockSpec(memory_space=pltpu.SMEM)
    return pl.pallas_call(
        body,
        out_shape=outs,
        in_specs=[smem] * len(scalars) + [vmem] * len(args),
        out_specs=[vmem] * len(outs),
        scratch_shapes=scratch,
        cost_estimate=pl.CostEstimate(flops=flops, bytes_accessed=flops // 256, transcendentals=0),
        compiler_params=pltpu.CompilerParams(vmem_limit_bytes=vmem_mib << 20),
    )(*scalars, *args)


def shaped(*shape):
    return jax.ShapeDtypeStruct(shape, F32)


def swap(value, axis, size, step):
    return lax.ppermute(value, axis, [(i, i ^ step) for i in range(size)])


def after(value, *others):
    return lax.optimization_barrier((value, *others))[0]


def entry_body(parts, info, ids, sensors, wq, wk, wv, packed, *refs):
    if packed is not None:
        packed[:, 0:LANES] = wq[...]
        packed[:, LANES : 2 * LANES] = wk[...]
        packed[:, 2 * LANES :] = wv[...]
    outs, rows = refs[:parts], refs[parts]
    count = sensors.shape[0]
    columns = outs[0].shape[1]
    local = ids[...] - info[2] * count
    chosen = lax.broadcasted_iota(jnp.int32, (count, count), 0) == local
    rows[...] = dot(chosen.astype(F32), sensors[...], NN)
    for r in range(parts):
        start = pl.multiple_of((info[2] ^ r) * columns, LANES)
        outs[r][...] = rows[:, pl.ds(start, columns)]


def entry(info, ids, sensors, weights, parts, direct):
    rows, columns = weights[0].shape
    count, width = sensors.shape

    def whole(*shape):
        return pl.BlockSpec(shape, lambda i, info: (0, 0))

    spec = pl.BlockSpec((rows, LANES), lambda i, info: (0, info[1]))
    body = entry_body if direct else adjoint_body
    outs = ([(rows, 3 * LANES)] if direct else []) + [(count, columns)] * parts
    return pl.pallas_call(
        functools.partial(body, parts),
        out_shape=[shaped(*o) for o in outs],
        grid_spec=pltpu.PrefetchScalarGridSpec(
            num_scalar_prefetch=1,
            grid=(1,),
            in_specs=[whole(1, count), whole(count, width)] + ([spec] * 3 if direct else []),
            out_specs=[whole(*o) for o in outs],
            scratch_shapes=[pltpu.VMEM((count, width), F32)],
        ),
        compiler_params=pltpu.CompilerParams(vmem_limit_bytes=60 << 20),
    )(info, ids, sensors, *(weights if direct else ()))


def columns_of(turn, info):
    return pl.ds(pl.multiple_of((info[1] ^ turn) * LANES, LANES), LANES)


def spread(held, axis, size):
    held, step = dict(held), size
    while step > 1:
        step //= 2
        if step not in held:
            held.update({r | step: swap(v, axis, size, step) for r, v in list(held.items())})
    return held


def adjoint_body(parts, info, ids, sensors, *refs):
    entry_body(parts, info, ids, sensors, None, None, None, None, *refs)


def stack_body(parts, *refs):
    rows = refs[0].shape[0]
    for r in range(parts):
        refs[parts][r * rows : (r + 1) * rows, :] = refs[r][...]


def attention_body(turn, blocks, wa, info, neighbours, *refs):
    x, wq, wk, wv = refs[:4]
    pieces = refs[4 : 3 + wa]
    adjoints = refs[3 + wa : 3 + wa + blocks]
    out, panel, proj = refs[3 + wa + blocks :]
    cols = columns_of(turn, info)
    count = wq.shape[0]

    def rows(r):
        return pl.ds(pl.multiple_of((info[0] ^ r) * count, 8), count)

    panel[rows(0), 0:LANES] = wq[:, cols]
    panel[rows(0), LANES : 2 * LANES] = wk[:, cols]
    panel[rows(0), 2 * LANES : 3 * LANES] = wv[:, cols]
    for r in range(1, wa):
        panel[rows(r), :] = pieces[r - 1][...]
    attention_core(cols, blocks, info[2], neighbours, x, panel, adjoints, out, proj)


def attention_panel_body(chunk, blocks, info, neighbours, x, panel, *refs):
    cols = slice(chunk * LANES, (chunk + 1) * LANES)
    attention_core(
        cols, blocks, info[2], neighbours, x, panel, refs[:blocks], refs[blocks], refs[blocks + 1]
    )


def attention_core(cols, blocks, t, neighbours, x, panel, adjoints, out, proj):
    proj[...] = dot(x[...], panel[...], NN)
    out[:, LANES:] = jnp.zeros((out.shape[0], 2 * LANES), F32)
    first = lax.broadcasted_iota(jnp.int32, (BLOCK, LANES), 1) < DH
    scale = DH ** (-0.5)

    def by_head(value):
        return jnp.concatenate(
            [jnp.where(first, value, 0.0), jnp.where(first, 0.0, value)], axis=0
        )

    for r in range(blocks):
        here = slice(r * BLOCK, (r + 1) * BLOCK)
        there = [
            pl.ds(pl.multiple_of((neighbours[t ^ r, j] ^ t) * BLOCK, BLOCK), BLOCK)
            for j in range(KB)
        ]
        query = by_head(proj[here, 0:LANES])
        adjoint = by_head(adjoints[r][:, cols])
        key = jnp.concatenate([proj[w, LANES : 2 * LANES] for w in there], axis=0)
        value = jnp.concatenate([proj[w, 2 * LANES :] for w in there], axis=0)
        scores = dot(query, key, NT) * scale
        raised = jnp.exp(scores - jnp.max(scores, axis=1, keepdims=True))
        attention = raised / jnp.sum(raised, axis=1, keepdims=True)
        weight_adjoint = dot(adjoint, value, NT)
        row_dots = jnp.sum(attention * weight_adjoint, axis=1, keepdims=True)
        score_adjoint = attention * (weight_adjoint - row_dots) * scale
        both = dot(score_adjoint, key, NN)
        out[here, 0:LANES] = jnp.where(first, both[:BLOCK], both[BLOCK:])
        dkey = dot(score_adjoint, query, TN)
        dvalue = dot(attention, adjoint, TN)
        for j, w in enumerate(there):
            part = slice(j * BLOCK, (j + 1) * BLOCK)
            out[w, LANES : 2 * LANES] += dkey[part]
            out[w, 2 * LANES :] += dvalue[part]


def weight_grad_body(shares, rows, info, x, stacked, out):
    for j, r in enumerate(shares):
        start = pl.multiple_of((info[0] ^ r) * rows, LANES)
        out[j * rows : (j + 1) * rows, :] = dot(x[:, pl.ds(start, rows)], stacked[...], TN)


def whole_grad_body(x, stacked, out):
    out[...] = dot(x[...], stacked[...], TN)


def back_body(shares, chunks, *refs):
    stacked, panels, out = refs[:chunks], refs[chunks : 2 * chunks], refs[2 * chunks]
    total = None
    for c in range(chunks):
        rows = jnp.concatenate(
            [stacked[c][r * BLOCK : (r + 1) * BLOCK, :] for r in shares], axis=0
        )
        term = dot(rows, panels[c][...], NT)
        total = term if total is None else total + term
    out[...] = total


def halve_body(rows, keep, got, send, kept):
    for j in range(keep.shape[0] // rows):
        out = send if j % 2 else kept
        place = slice(j // 2 * rows, (j // 2 + 1) * rows)
        here = slice(j * rows, (j + 1) * rows)
        out[place, :] = keep[here, :] + got[here, :]


def scatter_halving(send, keep, axis, size, rows):
    step, first = 1, None
    while True:
        got = swap(send, axis, size, step)
        step *= 2
        if step == size:
            return keep, got, first
        shape = shaped(keep.shape[0] // 2, keep.shape[1])
        send, keep = local_call(functools.partial(halve_body, rows), [shape] * 2, [keep, got])
        first = keep if first is None else first


def sum_body(rows, kept, got, out):
    out[...] = kept[-rows:, :] + got[-rows:, :]


def join_body(turns, info, *refs):
    count = (len(refs) - 3) // turns
    for turn in range(turns):
        for i in range(3):
            part = slice(i * LANES, (i + 1) * LANES)
            rows = refs[-1].shape[0]
            total = refs[turn * count][:rows, part]
            for term in refs[turn * count + 1 : (turn + 1) * count]:
                total += term[:rows, part]
            refs[turns * count + i][:, columns_of(turn, info)] = total


def per_device(sizes, node_features, sensor_adjoint, sensor_node, neighbours, *weights):
    grp, wa, ta = sizes
    hour_rows = node_features[0]
    nodes_here, width = hour_rows.shape
    rows_here, columns = weights[0].shape
    chunks = columns // LANES
    blocks = ta
    nodes = nodes_here * ta
    z, y, t = lax.axis_index("wa"), lax.axis_index("grp"), lax.axis_index("ta")
    info = jnp.stack([z, y, t]).astype(jnp.int32)
    direct = rows_here % LANES == 0 and chunks == grp == 2 and wa == 4

    blocks_out = entry(info, sensor_node.reshape(1, -1), sensor_adjoint[0], weights, ta, direct)
    held = {0: hour_rows}
    if direct:
        first, *blocks_out = blocks_out
        held[0] = after(hour_rows, first)
        gathered = [spread({0: first}, "wa", wa)]
        gathered.append({r: swap(gathered[0][r], "grp", grp, 1) for r in range(1, wa)})
        held[ta // 2] = after(swap(held[0], "ta", ta, ta // 2), gathered[0][1])
    held = spread(held, "ta", ta)
    adjoints = [blocks_out[0]] + [
        swap(after(blocks_out[r], held[ta // 2]), "ta", ta, r) for r in range(1, ta)
    ]
    inputs = local_call(
        functools.partial(stack_body, ta), [shaped(nodes, width)], [held[r] for r in range(ta)]
    )[0]

    stacked, panels, owned, sent, ready = [], [], [], [], []
    for c in range(chunks):
        proj_flops = 12 * nodes * width * 3 * LANES + 60 * 2 * nodes * 4 * BLOCK * LANES
        scratch = [pltpu.VMEM((nodes, 3 * LANES), F32)]
        turn = after(info, stacked[-1], *sent) if stacked else info
        if direct:
            dqkv, panel = local_call(
                functools.partial(attention_body, c, blocks, wa),
                [shaped(nodes, 3 * LANES), shaped(width, 3 * LANES)],
                [inputs, *weights, *[gathered[c][r] for r in range(1, wa)], *adjoints],
                scalars=[turn, neighbours],
                scratch=scratch,
                flops=proj_flops,
            )
            if not c:
                later = after(info, dqkv, *[gathered[1][r] for r in GATE])
                odd = grads_of((1, 3), later, inputs, dqkv, rows_here)
                even = grads_of((0, 2), after(info, odd), inputs, dqkv, rows_here)
                got = swap(odd, "wa", wa, 1)
                passed = total_of(even, got, rows_here)
                owned = [even, got, swap(passed, "wa", wa, 2)]
                sent = [odd]
            else:
                shares = {}
                for r in (3, 1, 2, 0):
                    shares[r] = grads_of((r,), after(info, *shares.values()), inputs, dqkv, rows_here)
                ready.append(shares)
        else:
            cols = slice(c * LANES, (c + 1) * LANES)
            local = jnp.concatenate([w[:, cols] for w in weights], axis=1)
            panel = lax.all_gather(local, "wa", axis=0, tiled=True)
            dqkv = local_call(
                functools.partial(attention_panel_body, c, blocks),
                [shaped(nodes, 3 * LANES)],
                [inputs, panel, *adjoints],
                scalars=[turn, neighbours],
                scratch=scratch,
                flops=proj_flops,
            )[0]
            full = local_call(whole_grad_body, [shaped(width, 3 * LANES)], [inputs, dqkv])[0]
            owned.append(lax.psum_scatter(full, "wa", scatter_dimension=0, tiled=True))
        stacked.append(dqkv)
        panels.append(panel)

    if direct:
        (shares,) = ready
        message = swap(after(shares[3], owned[1]), "wa", wa, 1)
        sent = [shares[3]]
    backs = [
        local_call(
            functools.partial(back_body, range(odd, ta, 2), chunks),
            [shaped(nodes // 2, width)],
            [*stacked, *[after(p, *sent) for p in panels]],
        )[0]
        for odd in (1, 0)
    ]
    backs[0] = after(backs[0], backs[1], shares[1], shares[2], message, owned[2]) if direct else backs[0]
    kept, got, early = scatter_halving(*backs, "ta", ta, nodes_here)
    if direct:
        wait = [owned[2]] + []
        passed = total_of(shares[2], after(message, *wait), rows_here)
        direct_got = swap(after(shares[1], message, *wait), "wa", wa, 1)
        owned += [shares[0], direct_got, swap(passed, "wa", wa, 2)]
    back = (kept + got)[None]
    if direct:
        grads = local_call(
            functools.partial(join_body, chunks),
            [shaped(rows_here, columns)] * 3,
            owned,
            scalars=[info],
        )
    else:
        grads = [
            jnp.concatenate([o[:, i * LANES : (i + 1) * LANES] for o in owned], axis=1)
            for i in range(3)
        ]
    return (back, *grads)


def solution(mesh):
    sizes = tuple(mesh.shape[name] for name in ("grp", "wa", "ta"))
    return jax.shard_map(
        functools.partial(per_device, sizes),
        mesh=mesh,
        in_specs=(
            P(("grp", "wa"), "ta", None),
            P(("grp", "wa"), "ta", None),
            P("ta"),
            P(),
            P("wa", "ta"),
            P("wa", "ta"),
            P("wa", "ta"),
        ),
        out_specs=(
            P(("grp", "wa"), "ta", None),
            P(("grp", "wa"), "ta"),
            P(("grp", "wa"), "ta"),
            P(("grp", "wa"), "ta"),
        ),
        check_vma=False,
    )
```

```python
import functools

import jax
import jax.numpy as jnp
from jax import lax
from jax.experimental import pallas as pl
from jax.experimental.pallas import tpu as pltpu
from jax.sharding import PartitionSpec as P

DH = 64
BLOCK = 128
KB = 2
GATE = ()
LANES = 128
F32 = jnp.float32
NN = ((1,), (0,))
NT = ((1,), (1,))
TN = ((0,), (0,))


def dot(left, right, dims):
    return lax.dot_general(
        left, right, (dims, ((), ())), precision=lax.Precision.HIGHEST, preferred_element_type=F32
    )


def grads_of(shares, info, inputs, stacked, rows):
    return local_call(
        functools.partial(weight_grad_body, shares, rows),
        [shaped(rows * len(shares), stacked.shape[1])],
        [inputs, stacked],
        scalars=[info],
    )[0]


def total_of(kept, got, rows):
    return local_call(
        functools.partial(sum_body, rows), [shaped(rows, kept.shape[1])], [kept, got]
    )[0]


def local_call(body, outs, args, scalars=(), scratch=(), flops=0, vmem_mib=24):
    vmem = pl.BlockSpec(memory_space=pltpu.VMEM)
    smem = pl.BlockSpec(memory_space=pltpu.SMEM)
    return pl.pallas_call(
        body,
        out_shape=outs,
        in_specs=[smem] * len(scalars) + [vmem] * len(args),
        out_specs=[vmem] * len(outs),
        scratch_shapes=scratch,
        cost_estimate=pl.CostEstimate(flops=flops, bytes_accessed=flops // 256, transcendentals=0),
        compiler_params=pltpu.CompilerParams(vmem_limit_bytes=vmem_mib << 20),
    )(*scalars, *args)


def shaped(*shape):
    return jax.ShapeDtypeStruct(shape, F32)


def swap(value, axis, size, step):
    return lax.ppermute(value, axis, [(i, i ^ step) for i in range(size)])


def after(value, *others):
    return lax.optimization_barrier((value, *others))[0]


def entry_body(parts, info, ids, sensors, wq, wk, wv, packed, *refs):
    if packed is not None:
        packed[:, 0:LANES] = wq[...]
        packed[:, LANES : 2 * LANES] = wk[...]
        packed[:, 2 * LANES :] = wv[...]
    outs, rows = refs[:parts], refs[parts]
    count = sensors.shape[0]
    columns = outs[0].shape[1]
    local = ids[...] - info[2] * count
    chosen = lax.broadcasted_iota(jnp.int32, (count, count), 0) == local
    rows[...] = dot(chosen.astype(F32), sensors[...], NN)
    for r in range(parts):
        start = pl.multiple_of((info[2] ^ r) * columns, LANES)
        outs[r][...] = rows[:, pl.ds(start, columns)]


def entry(info, ids, sensors, weights, parts, direct):
    rows, columns = weights[0].shape
    count, width = sensors.shape

    def whole(*shape):
        return pl.BlockSpec(shape, lambda i, info: (0, 0))

    spec = pl.BlockSpec((rows, LANES), lambda i, info: (0, info[1]))
    body = entry_body if direct else adjoint_body
    outs = ([(rows, 3 * LANES)] if direct else []) + [(count, columns)] * parts
    return pl.pallas_call(
        functools.partial(body, parts),
        out_shape=[shaped(*o) for o in outs],
        grid_spec=pltpu.PrefetchScalarGridSpec(
            num_scalar_prefetch=1,
            grid=(1,),
            in_specs=[whole(1, count), whole(count, width)] + ([spec] * 3 if direct else []),
            out_specs=[whole(*o) for o in outs],
            scratch_shapes=[pltpu.VMEM((count, width), F32)],
        ),
        compiler_params=pltpu.CompilerParams(vmem_limit_bytes=60 << 20),
    )(info, ids, sensors, *(weights if direct else ()))


def columns_of(turn, info):
    return pl.ds(pl.multiple_of((info[1] ^ turn) * LANES, LANES), LANES)


def spread(held, axis, size):
    held, step = dict(held), size
    while step > 1:
        step //= 2
        if step not in held:
            held.update({r | step: swap(v, axis, size, step) for r, v in list(held.items())})
    return held


def adjoint_body(parts, info, ids, sensors, *refs):
    entry_body(parts, info, ids, sensors, None, None, None, None, *refs)


def stack_body(parts, *refs):
    rows = refs[0].shape[0]
    for r in range(parts):
        refs[parts][r * rows : (r + 1) * rows, :] = refs[r][...]


def attention_body(turn, blocks, wa, info, neighbours, *refs):
    x, wq, wk, wv = refs[:4]
    pieces = refs[4 : 3 + wa]
    adjoints = refs[3 + wa : 3 + wa + blocks]
    out, panel, proj = refs[3 + wa + blocks :]
    cols = columns_of(turn, info)
    count = wq.shape[0]

    def rows(r):
        return pl.ds(pl.multiple_of((info[0] ^ r) * count, 8), count)

    panel[rows(0), 0:LANES] = wq[:, cols]
    panel[rows(0), LANES : 2 * LANES] = wk[:, cols]
    panel[rows(0), 2 * LANES : 3 * LANES] = wv[:, cols]
    for r in range(1, wa):
        panel[rows(r), :] = pieces[r - 1][...]
    attention_core(cols, blocks, info[2], neighbours, x, panel, adjoints, out, proj)


def attention_panel_body(chunk, blocks, info, neighbours, x, panel, *refs):
    cols = slice(chunk * LANES, (chunk + 1) * LANES)
    attention_core(
        cols, blocks, info[2], neighbours, x, panel, refs[:blocks], refs[blocks], refs[blocks + 1]
    )


BF16 = jnp.bfloat16


def halves_of(value):
    high = value.astype(BF16)
    return high, (value - high.astype(F32)).astype(BF16)


def dot_halves(left, right, dims):
    (high, low), (high_right, low_right) = left, right

    def term(one, other):
        return lax.dot_general(one, other, (dims, ((), ())), preferred_element_type=F32)

    return (term(high, low_right) + term(low, high_right)) + term(high, high_right)


def attention_core(cols, blocks, t, neighbours, x, panel, adjoints, out, proj):
    proj[...] = dot(x[...], panel[...], NN)
    out[:, LANES:] = jnp.zeros((out.shape[0], 2 * LANES), F32)
    first = lax.broadcasted_iota(jnp.int32, (BLOCK, LANES), 1) < DH
    scale = DH ** (-0.5)

    def by_head(value):
        return jnp.concatenate(
            [jnp.where(first, value, 0.0), jnp.where(first, 0.0, value)], axis=0
        )

    every = range(blocks)
    here = [slice(r * BLOCK, (r + 1) * BLOCK) for r in every]
    there = [
        [
            pl.ds(pl.multiple_of((neighbours[t ^ r, j] ^ t) * BLOCK, BLOCK), BLOCK)
            for j in range(KB)
        ]
        for r in every
    ]
    query = [by_head(proj[here[r], 0:LANES]) for r in every]
    adjoint = [by_head(adjoints[r][:, cols]) for r in every]
    key = [jnp.concatenate([proj[w, LANES : 2 * LANES] for w in there[r]], axis=0) for r in every]
    value = [jnp.concatenate([proj[w, 2 * LANES :] for w in there[r]], axis=0) for r in every]
    scores = [dot(query[r], key[r], NT) * scale for r in every]
    weight_adjoint = [dot(adjoint[r], value[r], NT) for r in every]
    raised = [jnp.exp(s - jnp.max(s, axis=1, keepdims=True)) for s in scores]
    attention = [v / jnp.sum(v, axis=1, keepdims=True) for v in raised]
    row_dots = [
        jnp.sum(attention[r] * weight_adjoint[r], axis=1, keepdims=True) for r in every
    ]
    score_adjoint = [
        halves_of(attention[r] * (weight_adjoint[r] - row_dots[r]) * scale) for r in every
    ]
    for r in every:
        dvalue = dot_halves(halves_of(attention[r]), halves_of(adjoint[r]), TN)
        both = dot_halves(score_adjoint[r], halves_of(key[r]), NN)
        out[here[r], 0:LANES] = jnp.where(first, both[:BLOCK], both[BLOCK:])
        dkey = dot_halves(score_adjoint[r], halves_of(query[r]), TN)
        for j, w in enumerate(there[r]):
            part = slice(j * BLOCK, (j + 1) * BLOCK)
            out[w, LANES : 2 * LANES] += dkey[part]
            out[w, 2 * LANES :] += dvalue[part]


def weight_grad_body(shares, rows, info, x, stacked, out):
    for j, r in enumerate(shares):
        start = pl.multiple_of((info[0] ^ r) * rows, LANES)
        out[j * rows : (j + 1) * rows, :] = dot(x[:, pl.ds(start, rows)], stacked[...], TN)


def whole_grad_body(x, stacked, out):
    out[...] = dot(x[...], stacked[...], TN)


def back_body(shares, chunks, *refs):
    stacked, panels, out = refs[:chunks], refs[chunks : 2 * chunks], refs[2 * chunks]
    total = None
    for c in range(chunks):
        rows = jnp.concatenate(
            [stacked[c][r * BLOCK : (r + 1) * BLOCK, :] for r in shares], axis=0
        )
        term = dot(rows, panels[c][...], NT)
        total = term if total is None else total + term
    out[...] = total


def halve_body(rows, keep, got, send, kept):
    for j in range(keep.shape[0] // rows):
        out = send if j % 2 else kept
        place = slice(j // 2 * rows, (j // 2 + 1) * rows)
        here = slice(j * rows, (j + 1) * rows)
        out[place, :] = keep[here, :] + got[here, :]


def scatter_halving(send, keep, axis, size, rows):
    step, first = 1, None
    while True:
        got = swap(send, axis, size, step)
        step *= 2
        if step == size:
            return keep, got, first
        shape = shaped(keep.shape[0] // 2, keep.shape[1])
        send, keep = local_call(functools.partial(halve_body, rows), [shape] * 2, [keep, got])
        first = keep if first is None else first


def sum_body(rows, kept, got, out):
    out[...] = kept[-rows:, :] + got[-rows:, :]


def join_body(turns, info, *refs):
    count = (len(refs) - 3) // turns
    for turn in range(turns):
        for i in range(3):
            part = slice(i * LANES, (i + 1) * LANES)
            rows = refs[-1].shape[0]
            total = refs[turn * count][:rows, part]
            for term in refs[turn * count + 1 : (turn + 1) * count]:
                total += term[:rows, part]
            refs[turns * count + i][:, columns_of(turn, info)] = total


def per_device(sizes, node_features, sensor_adjoint, sensor_node, neighbours, *weights):
    grp, wa, ta = sizes
    hour_rows = node_features[0]
    nodes_here, width = hour_rows.shape
    rows_here, columns = weights[0].shape
    chunks = columns // LANES
    blocks = ta
    nodes = nodes_here * ta
    z, y, t = lax.axis_index("wa"), lax.axis_index("grp"), lax.axis_index("ta")
    info = jnp.stack([z, y, t]).astype(jnp.int32)
    direct = rows_here % LANES == 0 and chunks == grp == 2 and wa == 4

    blocks_out = entry(info, sensor_node.reshape(1, -1), sensor_adjoint[0], weights, ta, direct)
    held = {0: hour_rows}
    if direct:
        first, *blocks_out = blocks_out
        held[0] = after(hour_rows, first)
        gathered = [spread({0: first}, "wa", wa)]
        gathered.append({r: swap(gathered[0][r], "grp", grp, 1) for r in range(1, wa)})
        held[ta // 2] = after(swap(held[0], "ta", ta, ta // 2), gathered[0][1])
    held = spread(held, "ta", ta)
    adjoints = [blocks_out[0]] + [
        swap(after(blocks_out[r], *[held[q] for q in range(1, ta)]), "ta", ta, r) for r in range(1, ta)
    ]
    inputs = local_call(
        functools.partial(stack_body, ta), [shaped(nodes, width)], [held[r] for r in range(ta)]
    )[0]

    stacked, panels, owned, sent, ready = [], [], [], [], []
    for c in range(chunks):
        proj_flops = 12 * nodes * width * 3 * LANES + 60 * 2 * nodes * 4 * BLOCK * LANES
        scratch = [pltpu.VMEM((nodes, 3 * LANES), F32)]
        turn = after(info, stacked[-1], *sent) if stacked else info
        if direct and not c:
            turn = after(turn, gathered[1][1])
        if direct:
            dqkv, panel = local_call(
                functools.partial(attention_body, c, blocks, wa),
                [shaped(nodes, 3 * LANES), shaped(width, 3 * LANES)],
                [inputs, *weights, *[gathered[c][r] for r in range(1, wa)], *adjoints],
                scalars=[turn, neighbours],
                scratch=scratch,
                flops=proj_flops,
            )
            if not c:
                later = after(info, dqkv, *[gathered[1][r] for r in GATE])
                odd = grads_of((1, 3), later, inputs, dqkv, rows_here)
                even = grads_of((0, 2), after(info, odd), inputs, dqkv, rows_here)
                got = swap(odd, "wa", wa, 1)
                passed = total_of(even, got, rows_here)
                owned = [even, got, swap(passed, "wa", wa, 2)]
                sent = [odd, even]
            else:
                shares = {}
                for r in (3, 1, 2, 0):
                    shares[r] = grads_of((r,), after(info, *shares.values()), inputs, dqkv, rows_here)
                ready.append(shares)
        else:
            cols = slice(c * LANES, (c + 1) * LANES)
            local = jnp.concatenate([w[:, cols] for w in weights], axis=1)
            panel = lax.all_gather(local, "wa", axis=0, tiled=True)
            dqkv = local_call(
                functools.partial(attention_panel_body, c, blocks),
                [shaped(nodes, 3 * LANES)],
                [inputs, panel, *adjoints],
                scalars=[turn, neighbours],
                scratch=scratch,
                flops=proj_flops,
            )[0]
            full = local_call(whole_grad_body, [shaped(width, 3 * LANES)], [inputs, dqkv])[0]
            owned.append(lax.psum_scatter(full, "wa", scatter_dimension=0, tiled=True))
        stacked.append(dqkv)
        panels.append(panel)

    if direct:
        (shares,) = ready
        message = swap(shares[3], "wa", wa, 1)
        sent = [shares[3]]
    backs = [
        local_call(
            functools.partial(back_body, range(odd, ta, 2), chunks),
            [shaped(nodes // 2, width)],
            [*stacked, *[after(p, *sent) for p in panels]],
        )[0]
        for odd in (1, 0)
    ]
    kept, got, early = scatter_halving(*backs, "ta", ta, nodes_here)
    if direct:
        wait = [owned[2]] + ([early] if early is not None else [])
        passed = total_of(shares[2], after(message, *wait), rows_here)
        direct_got = swap(after(shares[1], message), "wa", wa, 1)
        owned += [shares[0], direct_got, swap(passed, "wa", wa, 2)]
    back = (kept + got)[None]
    if direct:
        grads = local_call(
            functools.partial(join_body, chunks),
            [shaped(rows_here, columns)] * 3,
            owned,
            scalars=[info],
        )
    else:
        grads = [
            jnp.concatenate([o[:, i * LANES : (i + 1) * LANES] for o in owned], axis=1)
            for i in range(3)
        ]
    return (back, *grads)


def solution(mesh):
    sizes = tuple(mesh.shape[name] for name in ("grp", "wa", "ta"))
    return jax.shard_map(
        functools.partial(per_device, sizes),
        mesh=mesh,
        in_specs=(
            P(("grp", "wa"), "ta", None),
            P(("grp", "wa"), "ta", None),
            P("ta"),
            P(),
            P("wa", "ta"),
            P("wa", "ta"),
            P("wa", "ta"),
        ),
        out_specs=(
            P(("grp", "wa"), "ta", None),
            P(("grp", "wa"), "ta"),
            P(("grp", "wa"), "ta"),
            P(("grp", "wa"), "ta"),
        ),
        check_vma=False,
    )
```

```python
import functools

import jax
import jax.numpy as jnp
from jax import lax
from jax.experimental import pallas as pl
from jax.experimental.pallas import tpu as pltpu
from jax.sharding import PartitionSpec as P

DH = 64
BLOCK = 128
KB = 2
GATE = ()
LANES = 128
F32 = jnp.float32
NN = ((1,), (0,))
NT = ((1,), (1,))
TN = ((0,), (0,))


def dot(left, right, dims):
    return lax.dot_general(
        left, right, (dims, ((), ())), precision=lax.Precision.HIGHEST, preferred_element_type=F32
    )


def grads_of(shares, info, inputs, stacked, rows):
    return local_call(
        functools.partial(weight_grad_body, shares, rows),
        [shaped(rows * len(shares), stacked.shape[1])],
        [inputs, stacked],
        scalars=[info],
    )[0]


def total_of(kept, got, rows):
    return local_call(
        functools.partial(sum_body, rows), [shaped(rows, kept.shape[1])], [kept, got]
    )[0]


def local_call(body, outs, args, scalars=(), scratch=(), flops=0, vmem_mib=24):
    vmem = pl.BlockSpec(memory_space=pltpu.VMEM)
    smem = pl.BlockSpec(memory_space=pltpu.SMEM)
    return pl.pallas_call(
        body,
        out_shape=outs,
        in_specs=[smem] * len(scalars) + [vmem] * len(args),
        out_specs=[vmem] * len(outs),
        scratch_shapes=scratch,
        cost_estimate=pl.CostEstimate(flops=flops, bytes_accessed=flops // 256, transcendentals=0),
        compiler_params=pltpu.CompilerParams(vmem_limit_bytes=vmem_mib << 20),
    )(*scalars, *args)


def shaped(*shape):
    return jax.ShapeDtypeStruct(shape, F32)


def swap(value, axis, size, step):
    return lax.ppermute(value, axis, [(i, i ^ step) for i in range(size)])


def after(value, *others):
    return lax.optimization_barrier((value, *others))[0]


def entry_body(parts, info, ids, sensors, wq, wk, wv, packed, *refs):
    if packed is not None:
        packed[:, 0:LANES] = wq[...]
        packed[:, LANES : 2 * LANES] = wk[...]
        packed[:, 2 * LANES :] = wv[...]
    outs, rows = refs[:parts], refs[parts]
    count = sensors.shape[0]
    columns = outs[0].shape[1]
    local = ids[...] - info[2] * count
    chosen = lax.broadcasted_iota(jnp.int32, (count, count), 0) == local
    rows[...] = dot(chosen.astype(F32), sensors[...], NN)
    for r in range(parts):
        start = pl.multiple_of((info[2] ^ r) * columns, LANES)
        outs[r][...] = rows[:, pl.ds(start, columns)]


def entry(info, ids, sensors, weights, parts, direct):
    rows, columns = weights[0].shape
    count, width = sensors.shape

    def whole(*shape):
        return pl.BlockSpec(shape, lambda i, info: (0, 0))

    spec = pl.BlockSpec((rows, LANES), lambda i, info: (0, info[1]))
    body = entry_body if direct else adjoint_body
    outs = ([(rows, 3 * LANES)] if direct else []) + [(count, columns)] * parts
    return pl.pallas_call(
        functools.partial(body, parts),
        out_shape=[shaped(*o) for o in outs],
        grid_spec=pltpu.PrefetchScalarGridSpec(
            num_scalar_prefetch=1,
            grid=(1,),
            in_specs=[whole(1, count), whole(count, width)] + ([spec] * 3 if direct else []),
            out_specs=[whole(*o) for o in outs],
            scratch_shapes=[pltpu.VMEM((count, width), F32)],
        ),
        compiler_params=pltpu.CompilerParams(vmem_limit_bytes=60 << 20),
    )(info, ids, sensors, *(weights if direct else ()))


def columns_of(turn, info):
    return pl.ds(pl.multiple_of((info[1] ^ turn) * LANES, LANES), LANES)


def spread(held, axis, size):
    held, step = dict(held), size
    while step > 1:
        step //= 2
        if step not in held:
            held.update({r | step: swap(v, axis, size, step) for r, v in list(held.items())})
    return held


def adjoint_body(parts, info, ids, sensors, *refs):
    entry_body(parts, info, ids, sensors, None, None, None, None, *refs)


def stack_body(parts, *refs):
    rows = refs[0].shape[0]
    for r in range(parts):
        refs[parts][r * rows : (r + 1) * rows, :] = refs[r][...]


def attention_body(turn, blocks, wa, info, neighbours, *refs):
    own = 1 if turn == 0 else 3
    x, *weights = refs[: 1 + own]
    pieces = refs[1 + own : own + wa]
    adjoints = refs[own + wa : own + wa + blocks]
    *parts, out, panel, proj = refs[own + wa + blocks :]
    cols = columns_of(turn, info)
    count = weights[0].shape[0]

    def rows(r):
        return pl.ds(pl.multiple_of((info[0] ^ r) * count, 8), count)

    if turn == 0:
        panel[rows(0), :] = weights[0][...]
    else:
        for i, weight in enumerate(weights):
            panel[rows(0), i * LANES : (i + 1) * LANES] = weight[:, cols]
    for r in range(1, wa):
        panel[rows(r), :] = pieces[r - 1][...]
    if parts:
        last = pl.ds(pl.multiple_of((info[0] ^ (wa - 1)) * count, LANES), count)
        proj[...] = parts[0][...] + dot(x[:, last], pieces[-1][...], NN)
    else:
        proj[...] = dot(x[...], panel[...], NN)
    attention_core(cols, blocks, info[2], neighbours, adjoints, out, proj)


def partial_body(info, x, *refs):
    *pieces, out = refs
    total = None
    for r, piece in enumerate(pieces):
        count = piece.shape[0]
        here = pl.ds(pl.multiple_of((info[0] ^ r) * count, LANES), count)
        term = dot(x[:, here], piece[...], NN)
        total = term if total is None else total + term
    out[...] = total


def attention_panel_body(chunk, blocks, info, neighbours, x, panel, *refs):
    cols = slice(chunk * LANES, (chunk + 1) * LANES)
    refs[blocks + 1][...] = dot(x[...], panel[...], NN)
    attention_core(cols, blocks, info[2], neighbours, refs[:blocks], *refs[blocks:])


BF16 = jnp.bfloat16


def halves_of(value):
    high = value.astype(BF16)
    return high, (value - high.astype(F32)).astype(BF16)


def dot_halves(left, right, dims):
    (high, low), (high_right, low_right) = left, right

    def term(one, other):
        return lax.dot_general(one, other, (dims, ((), ())), preferred_element_type=F32)

    return (term(high, low_right) + term(low, high_right)) + term(high, high_right)


def attention_core(cols, blocks, t, neighbours, adjoints, out, proj):
    out[:, LANES:] = jnp.zeros((out.shape[0], 2 * LANES), F32)
    first = lax.broadcasted_iota(jnp.int32, (BLOCK, LANES), 1) < DH
    scale = DH ** (-0.5)

    def by_head(value):
        return jnp.concatenate(
            [jnp.where(first, value, 0.0), jnp.where(first, 0.0, value)], axis=0
        )

    every = range(blocks)
    here = [slice(r * BLOCK, (r + 1) * BLOCK) for r in every]
    there = [
        [
            pl.ds(pl.multiple_of((neighbours[t ^ r, j] ^ t) * BLOCK, BLOCK), BLOCK)
            for j in range(KB)
        ]
        for r in every
    ]
    query = [by_head(proj[here[r], 0:LANES]) for r in every]
    adjoint = [by_head(adjoints[r][:, cols]) for r in every]
    key = [jnp.concatenate([proj[w, LANES : 2 * LANES] for w in there[r]], axis=0) for r in every]
    value = [jnp.concatenate([proj[w, 2 * LANES :] for w in there[r]], axis=0) for r in every]
    scores = [dot(query[r], key[r], NT) * scale for r in every]
    weight_adjoint = [dot(adjoint[r], value[r], NT) for r in every]
    raised = [jnp.exp(s - jnp.max(s, axis=1, keepdims=True)) for s in scores]
    attention = [v / jnp.sum(v, axis=1, keepdims=True) for v in raised]
    row_dots = [
        jnp.sum(attention[r] * weight_adjoint[r], axis=1, keepdims=True) for r in every
    ]
    score_adjoint = [
        halves_of(attention[r] * (weight_adjoint[r] - row_dots[r]) * scale) for r in every
    ]
    for r in every:
        dvalue = dot_halves(halves_of(attention[r]), halves_of(adjoint[r]), TN)
        both = dot_halves(score_adjoint[r], halves_of(key[r]), NN)
        out[here[r], 0:LANES] = jnp.where(first, both[:BLOCK], both[BLOCK:])
        dkey = dot_halves(score_adjoint[r], halves_of(query[r]), TN)
        for j, w in enumerate(there[r]):
            part = slice(j * BLOCK, (j + 1) * BLOCK)
            out[w, LANES : 2 * LANES] += dkey[part]
            out[w, 2 * LANES :] += dvalue[part]


def weight_grad_body(shares, rows, info, x, stacked, out):
    for j, r in enumerate(shares):
        start = pl.multiple_of((info[0] ^ r) * rows, LANES)
        out[j * rows : (j + 1) * rows, :] = dot(x[:, pl.ds(start, rows)], stacked[...], TN)


def whole_grad_body(x, stacked, out):
    out[...] = dot(x[...], stacked[...], TN)


def back_body(shares, chunks, *refs):
    stacked, panels, out = refs[:chunks], refs[chunks : 2 * chunks], refs[2 * chunks]
    total = None
    for c in range(chunks):
        rows = jnp.concatenate(
            [stacked[c][r * BLOCK : (r + 1) * BLOCK, :] for r in shares], axis=0
        )
        term = dot(rows, panels[c][...], NT)
        total = term if total is None else total + term
    out[...] = total


def halve_body(rows, keep, got, send, kept):
    for j in range(keep.shape[0] // rows):
        out = send if j % 2 else kept
        place = slice(j // 2 * rows, (j // 2 + 1) * rows)
        here = slice(j * rows, (j + 1) * rows)
        out[place, :] = keep[here, :] + got[here, :]


def scatter_halving(send, keep, axis, size, rows):
    step, first = 1, None
    while True:
        got = swap(send, axis, size, step)
        step *= 2
        if step == size:
            return keep, got, first
        shape = shaped(keep.shape[0] // 2, keep.shape[1])
        send, keep = local_call(functools.partial(halve_body, rows), [shape] * 2, [keep, got])
        first = keep if first is None else first


def sum_body(rows, kept, got, out):
    out[...] = kept[-rows:, :] + got[-rows:, :]


def join_body(turns, info, *refs):
    *refs, back = refs
    count = (len(refs) - 5) // turns
    back[...] = refs[turns * count][...] + refs[turns * count + 1][...]
    outs = refs[turns * count + 2 :]
    for turn in range(turns):
        for i in range(3):
            part = slice(i * LANES, (i + 1) * LANES)
            rows = outs[0].shape[0]
            total = refs[turn * count][:rows, part]
            for term in refs[turn * count + 1 : (turn + 1) * count]:
                total += term[:rows, part]
            outs[i][:, columns_of(turn, info)] = total


def per_device(sizes, node_features, sensor_adjoint, sensor_node, neighbours, *weights):
    grp, wa, ta = sizes
    hour_rows = node_features[0]
    nodes_here, width = hour_rows.shape
    rows_here, columns = weights[0].shape
    chunks = columns // LANES
    blocks = ta
    nodes = nodes_here * ta
    z, y, t = lax.axis_index("wa"), lax.axis_index("grp"), lax.axis_index("ta")
    info = jnp.stack([z, y, t]).astype(jnp.int32)
    direct = rows_here % LANES == 0 and chunks == grp == 2 and wa == 4

    blocks_out = entry(info, sensor_node.reshape(1, -1), sensor_adjoint[0], weights, ta, direct)
    held = {0: hour_rows}
    if direct:
        first, *blocks_out = blocks_out
        held[0] = after(hour_rows, first)
        gathered = [spread({0: first}, "wa", wa)]
        gathered.append({1: swap(gathered[0][1], "grp", grp, 1)})
        held[ta // 2] = after(swap(held[0], "ta", ta, ta // 2), gathered[0][1])
    held = spread(held, "ta", ta)
    adjoints = [blocks_out[0]] + [
        swap(after(blocks_out[r], *[held[q] for q in range(1, ta)]), "ta", ta, r) for r in range(1, ta)
    ]
    inputs = local_call(
        functools.partial(stack_body, ta), [shaped(nodes, width)], [held[r] for r in range(ta)]
    )[0]

    parts = []
    if direct:
        parts = local_call(
            partial_body,
            [shaped(nodes, 3 * LANES)],
            [inputs, *[gathered[0][r] for r in range(wa - 1)]],
            scalars=[info],
        )
        gathered[1][2] = swap(after(gathered[0][2], *parts, gathered[1][1]), "grp", grp, 1)
        gathered[1][3] = swap(gathered[0][3], "grp", grp, 1)

    stacked, panels, owned, sent, ready = [], [], [], [], []
    for c in range(chunks):
        proj_flops = 12 * nodes * width * 3 * LANES + 60 * 2 * nodes * 4 * BLOCK * LANES
        scratch = [pltpu.VMEM((nodes, 3 * LANES), F32)]
        turn = after(info, stacked[-1], *sent) if stacked else info
        if direct:
            dqkv, panel = local_call(
                functools.partial(attention_body, c, blocks, wa),
                [shaped(nodes, 3 * LANES), shaped(width, 3 * LANES)],
                [
                    inputs,
                    *(weights if c else [first]),
                    *[gathered[c][r] for r in range(1, wa)],
                    *adjoints,
                    *([] if c else parts),
                ],
                scalars=[turn, neighbours],
                scratch=scratch,
                flops=proj_flops,
            )
            if not c:
                later = after(info, dqkv, *[gathered[1][r] for r in GATE])
                odd = grads_of((1, 3), later, inputs, dqkv, rows_here)
                even = grads_of((0, 2), after(info, odd), inputs, dqkv, rows_here)
                got = swap(odd, "wa", wa, 1)
                passed = total_of(even, got, rows_here)
                owned = [even, got, swap(passed, "wa", wa, 2)]
                sent = [odd, even]
            else:
                shares = {}
                for r in (3, 1, 2, 0):
                    shares[r] = grads_of((r,), after(info, *shares.values()), inputs, dqkv, rows_here)
                ready.append(shares)
        else:
            cols = slice(c * LANES, (c + 1) * LANES)
            local = jnp.concatenate([w[:, cols] for w in weights], axis=1)
            panel = lax.all_gather(local, "wa", axis=0, tiled=True)
            dqkv = local_call(
                functools.partial(attention_panel_body, c, blocks),
                [shaped(nodes, 3 * LANES)],
                [inputs, panel, *adjoints],
                scalars=[turn, neighbours],
                scratch=scratch,
                flops=proj_flops,
            )[0]
            full = local_call(whole_grad_body, [shaped(width, 3 * LANES)], [inputs, dqkv])[0]
            owned.append(lax.psum_scatter(full, "wa", scatter_dimension=0, tiled=True))
        stacked.append(dqkv)
        panels.append(panel)

    if direct:
        (shares,) = ready
        message = swap(shares[3], "wa", wa, 1)
        sent = [shares[3]]
    backs = [
        local_call(
            functools.partial(back_body, range(odd, ta, 2), chunks),
            [shaped(nodes // 2, width)],
            [*stacked, *[after(p, *sent) for p in panels]],
        )[0]
        for odd in (1, 0)
    ]
    kept, got, early = scatter_halving(*backs, "ta", ta, nodes_here)
    if direct:
        wait = [owned[2]] + ([early] if early is not None else [])
        passed = total_of(shares[2], after(message, *wait), rows_here)
        direct_got = swap(after(shares[1], message), "wa", wa, 1)
        owned += [shares[0], direct_got, swap(passed, "wa", wa, 2)]
    if direct:
        *grads, back = local_call(
            functools.partial(join_body, chunks),
            [shaped(rows_here, columns)] * 3 + [shaped(nodes_here, width)],
            [*owned, kept, got],
            scalars=[info],
        )
    else:
        back = kept + got
        grads = [
            jnp.concatenate([o[:, i * LANES : (i + 1) * LANES] for o in owned], axis=1)
            for i in range(3)
        ]
    return (back[None], *grads)


def solution(mesh):
    sizes = tuple(mesh.shape[name] for name in ("grp", "wa", "ta"))
    return jax.shard_map(
        functools.partial(per_device, sizes),
        mesh=mesh,
        in_specs=(
            P(("grp", "wa"), "ta", None),
            P(("grp", "wa"), "ta", None),
            P("ta"),
            P(),
            P("wa", "ta"),
            P("wa", "ta"),
            P("wa", "ta"),
        ),
        out_specs=(
            P(("grp", "wa"), "ta", None),
            P(("grp", "wa"), "ta"),
            P(("grp", "wa"), "ta"),
            P(("grp", "wa"), "ta"),
        ),
        check_vma=False,
    )
```

```python
import functools

import jax
import jax.numpy as jnp
from jax import lax
from jax.experimental import pallas as pl
from jax.experimental.pallas import tpu as pltpu
from jax.sharding import PartitionSpec as P

DH = 64
BLOCK = 128
KB = 2
GATE = ()
LANES = 128
F32 = jnp.float32
NN = ((1,), (0,))
NT = ((1,), (1,))
TN = ((0,), (0,))


def dot(left, right, dims):
    return lax.dot_general(
        left, right, (dims, ((), ())), precision=lax.Precision.HIGHEST, preferred_element_type=F32
    )


def grads_of(shares, info, inputs, stacked, rows):
    return local_call(
        functools.partial(weight_grad_body, shares, rows),
        [shaped(rows * len(shares), stacked.shape[1])],
        [inputs, stacked],
        scalars=[info],
    )[0]


def total_of(kept, got, rows):
    return local_call(
        functools.partial(sum_body, rows), [shaped(rows, kept.shape[1])], [kept, got]
    )[0]


def local_call(body, outs, args, scalars=(), scratch=(), flops=0, vmem_mib=24):
    vmem = pl.BlockSpec(memory_space=pltpu.VMEM)
    smem = pl.BlockSpec(memory_space=pltpu.SMEM)
    return pl.pallas_call(
        body,
        out_shape=outs,
        in_specs=[smem] * len(scalars) + [vmem] * len(args),
        out_specs=[vmem] * len(outs),
        scratch_shapes=scratch,
        cost_estimate=pl.CostEstimate(flops=flops, bytes_accessed=flops // 256, transcendentals=0),
        compiler_params=pltpu.CompilerParams(vmem_limit_bytes=vmem_mib << 20),
    )(*scalars, *args)


def shaped(*shape):
    return jax.ShapeDtypeStruct(shape, F32)


def swap(value, axis, size, step):
    return lax.ppermute(value, axis, [(i, i ^ step) for i in range(size)])


def after(value, *others):
    return lax.optimization_barrier((value, *others))[0]


def entry_body(parts, ids, sensors, wq, wk, wv, packed, *refs):
    mine = lax.axis_index("ta")
    if packed is not None:
        packed[:, 0:LANES] = wq[...]
        packed[:, LANES : 2 * LANES] = wk[...]
        packed[:, 2 * LANES :] = wv[...]
    outs, rows = refs[:parts], refs[parts]
    count = sensors.shape[0]
    columns = outs[0].shape[1]
    local = ids[...] - mine * count
    chosen = lax.broadcasted_iota(jnp.int32, (count, count), 0) == local
    rows[...] = dot(chosen.astype(F32), sensors[...], NN)
    for r in range(parts):
        start = pl.multiple_of((mine ^ r) * columns, LANES)
        outs[r][...] = rows[:, pl.ds(start, columns)]


def entry(ids, sensors, weights, parts, direct):
    rows, columns = weights[0].shape
    count, width = sensors.shape

    def whole(*shape):
        return pl.BlockSpec(shape, lambda i: (0, 0))

    spec = pl.BlockSpec((rows, LANES), lambda i: (0, lax.axis_index("grp")))
    body = entry_body if direct else adjoint_body
    outs = ([(rows, 3 * LANES)] if direct else []) + [(count, columns)] * parts
    return pl.pallas_call(
        functools.partial(body, parts),
        out_shape=[shaped(*o) for o in outs],
        grid_spec=pltpu.PrefetchScalarGridSpec(
            num_scalar_prefetch=0,
            grid=(1,),
            in_specs=[whole(1, count), whole(count, width)] + ([spec] * 3 if direct else []),
            out_specs=[whole(*o) for o in outs],
            scratch_shapes=[pltpu.VMEM((count, width), F32)],
        ),
        compiler_params=pltpu.CompilerParams(vmem_limit_bytes=60 << 20),
    )(ids, sensors, *(weights if direct else ()))


def columns_of(turn, info):
    return pl.ds(pl.multiple_of((info[1] ^ turn) * LANES, LANES), LANES)


def spread(held, axis, size):
    held, step = dict(held), size
    while step > 1:
        step //= 2
        if step not in held:
            held.update({r | step: swap(v, axis, size, step) for r, v in list(held.items())})
    return held


def adjoint_body(parts, ids, sensors, *refs):
    entry_body(parts, ids, sensors, None, None, None, None, *refs)


def stack_body(parts, *refs):
    rows = refs[0].shape[0]
    for r in range(parts):
        refs[parts][r * rows : (r + 1) * rows, :] = refs[r][...]


def attention_body(turn, blocks, wa, info, neighbours, *refs):
    own = 1 if turn == 0 else 3
    x, *weights = refs[: 1 + own]
    pieces = refs[1 + own : own + wa]
    adjoints = refs[own + wa : own + wa + blocks]
    *parts, out, panel, proj = refs[own + wa + blocks :]
    cols = columns_of(turn, info)
    count = weights[0].shape[0]

    def rows(r):
        return pl.ds(pl.multiple_of((info[0] ^ r) * count, 8), count)

    if turn == 0:
        panel[rows(0), :] = weights[0][...]
    else:
        for i, weight in enumerate(weights):
            panel[rows(0), i * LANES : (i + 1) * LANES] = weight[:, cols]
    for r in range(1, wa):
        panel[rows(r), :] = pieces[r - 1][...]
    if parts:
        last = pl.ds(pl.multiple_of((info[0] ^ (wa - 1)) * count, LANES), count)
        proj[...] = parts[0][...] + dot(x[:, last], pieces[-1][...], NN)
    else:
        proj[...] = dot(x[...], panel[...], NN)
    attention_core(cols, blocks, info[2], neighbours, adjoints, out, proj)


def partial_body(info, x, *refs):
    *pieces, out = refs
    total = None
    for r, piece in enumerate(pieces):
        count = piece.shape[0]
        here = pl.ds(pl.multiple_of((info[0] ^ r) * count, LANES), count)
        term = dot(x[:, here], piece[...], NN)
        total = term if total is None else total + term
    out[...] = total


def attention_panel_body(chunk, blocks, info, neighbours, x, panel, *refs):
    cols = slice(chunk * LANES, (chunk + 1) * LANES)
    refs[blocks + 1][...] = dot(x[...], panel[...], NN)
    attention_core(cols, blocks, info[2], neighbours, refs[:blocks], *refs[blocks:])


BF16 = jnp.bfloat16


def halves_of(value):
    high = value.astype(BF16)
    return high, (value - high.astype(F32)).astype(BF16)


def dot_halves(left, right, dims):
    (high, low), (high_right, low_right) = left, right

    def term(one, other):
        return lax.dot_general(one, other, (dims, ((), ())), preferred_element_type=F32)

    return (term(high, low_right) + term(low, high_right)) + term(high, high_right)


def attention_core(cols, blocks, t, neighbours, adjoints, out, proj):
    out[:, LANES:] = jnp.zeros((out.shape[0], 2 * LANES), F32)
    first = lax.broadcasted_iota(jnp.int32, (BLOCK, LANES), 1) < DH
    scale = DH ** (-0.5)

    def by_head(value):
        return jnp.concatenate(
            [jnp.where(first, value, 0.0), jnp.where(first, 0.0, value)], axis=0
        )

    every = range(blocks)
    here = [slice(r * BLOCK, (r + 1) * BLOCK) for r in every]
    there = [
        [
            pl.ds(pl.multiple_of((neighbours[t ^ r, j] ^ t) * BLOCK, BLOCK), BLOCK)
            for j in range(KB)
        ]
        for r in every
    ]
    query = [by_head(proj[here[r], 0:LANES]) for r in every]
    adjoint = [by_head(adjoints[r][:, cols]) for r in every]
    key = [jnp.concatenate([proj[w, LANES : 2 * LANES] for w in there[r]], axis=0) for r in every]
    value = [jnp.concatenate([proj[w, 2 * LANES :] for w in there[r]], axis=0) for r in every]
    scores = [dot(query[r], key[r], NT) * scale for r in every]
    weight_adjoint = [dot(adjoint[r], value[r], NT) for r in every]
    raised = [jnp.exp(s - jnp.max(s, axis=1, keepdims=True)) for s in scores]
    attention = [v / jnp.sum(v, axis=1, keepdims=True) for v in raised]
    row_dots = [
        jnp.sum(attention[r] * weight_adjoint[r], axis=1, keepdims=True) for r in every
    ]
    score_adjoint = [
        halves_of(attention[r] * (weight_adjoint[r] - row_dots[r]) * scale) for r in every
    ]
    for r in every:
        dvalue = dot_halves(halves_of(attention[r]), halves_of(adjoint[r]), TN)
        both = dot_halves(score_adjoint[r], halves_of(key[r]), NN)
        out[here[r], 0:LANES] = jnp.where(first, both[:BLOCK], both[BLOCK:])
        dkey = dot_halves(score_adjoint[r], halves_of(query[r]), TN)
        for j, w in enumerate(there[r]):
            part = slice(j * BLOCK, (j + 1) * BLOCK)
            out[w, LANES : 2 * LANES] += dkey[part]
            out[w, 2 * LANES :] += dvalue[part]


def weight_grad_body(shares, rows, info, x, stacked, out):
    for j, r in enumerate(shares):
        start = pl.multiple_of((info[0] ^ r) * rows, LANES)
        out[j * rows : (j + 1) * rows, :] = dot(x[:, pl.ds(start, rows)], stacked[...], TN)


def whole_grad_body(x, stacked, out):
    out[...] = dot(x[...], stacked[...], TN)


def back_body(shares, chunks, *refs):
    stacked, panels, out = refs[:chunks], refs[chunks : 2 * chunks], refs[2 * chunks]
    total = None
    for c in range(chunks):
        rows = jnp.concatenate(
            [stacked[c][r * BLOCK : (r + 1) * BLOCK, :] for r in shares], axis=0
        )
        term = dot(rows, panels[c][...], NT)
        total = term if total is None else total + term
    out[...] = total


def halve_body(rows, keep, got, send, kept):
    for j in range(keep.shape[0] // rows):
        out = send if j % 2 else kept
        place = slice(j // 2 * rows, (j // 2 + 1) * rows)
        here = slice(j * rows, (j + 1) * rows)
        out[place, :] = keep[here, :] + got[here, :]


def scatter_halving(send, keep, axis, size, rows):
    step, first = 1, None
    while True:
        got = swap(send, axis, size, step)
        step *= 2
        if step == size:
            return keep, got, first
        shape = shaped(keep.shape[0] // 2, keep.shape[1])
        send, keep = local_call(functools.partial(halve_body, rows), [shape] * 2, [keep, got])
        first = keep if first is None else first


def sum_body(rows, kept, got, out):
    out[...] = kept[-rows:, :] + got[-rows:, :]


def join_body(turns, info, *refs):
    *refs, back = refs
    count = (len(refs) - 5) // turns
    back[...] = refs[turns * count][...] + refs[turns * count + 1][...]
    outs = refs[turns * count + 2 :]
    for turn in range(turns):
        for i in range(3):
            part = slice(i * LANES, (i + 1) * LANES)
            rows = outs[0].shape[0]
            total = refs[turn * count][:rows, part]
            for term in refs[turn * count + 1 : (turn + 1) * count]:
                total += term[:rows, part]
            outs[i][:, columns_of(turn, info)] = total


def per_device(sizes, node_features, sensor_adjoint, sensor_node, neighbours, *weights):
    grp, wa, ta = sizes
    hour_rows = node_features[0]
    nodes_here, width = hour_rows.shape
    rows_here, columns = weights[0].shape
    chunks = columns // LANES
    blocks = ta
    nodes = nodes_here * ta
    z, y, t = lax.axis_index("wa"), lax.axis_index("grp"), lax.axis_index("ta")
    info = jnp.stack([z, y, t]).astype(jnp.int32)
    direct = rows_here % LANES == 0 and chunks == grp == 2 and wa == 4

    blocks_out = entry(sensor_node.reshape(1, -1), sensor_adjoint[0], weights, ta, direct)
    held = {0: hour_rows}
    if direct:
        first, *blocks_out = blocks_out
        held[0] = after(hour_rows, first)
        gathered = [spread({0: first}, "wa", wa)]
        gathered.append({1: swap(gathered[0][1], "grp", grp, 1)})
        held[ta // 2] = after(swap(held[0], "ta", ta, ta // 2), gathered[0][1])
    held = spread(held, "ta", ta)
    adjoints = [blocks_out[0]] + [
        swap(after(blocks_out[r], *[held[q] for q in range(1, ta)]), "ta", ta, r) for r in range(1, ta)
    ]
    inputs = local_call(
        functools.partial(stack_body, ta), [shaped(nodes, width)], [held[r] for r in range(ta)]
    )[0]

    parts = []
    if direct:
        parts = local_call(
            partial_body,
            [shaped(nodes, 3 * LANES)],
            [inputs, *[gathered[0][r] for r in range(wa - 1)]],
            scalars=[info],
        )
        gathered[1][2] = swap(after(gathered[0][2], *parts, gathered[1][1]), "grp", grp, 1)
        gathered[1][3] = swap(gathered[0][3], "grp", grp, 1)

    stacked, panels, owned, sent, ready = [], [], [], [], []
    for c in range(chunks):
        proj_flops = 12 * nodes * width * 3 * LANES + 60 * 2 * nodes * 4 * BLOCK * LANES
        scratch = [pltpu.VMEM((nodes, 3 * LANES), F32)]
        turn = after(info, stacked[-1], *sent) if stacked else info
        if direct:
            dqkv, panel = local_call(
                functools.partial(attention_body, c, blocks, wa),
                [shaped(nodes, 3 * LANES), shaped(width, 3 * LANES)],
                [
                    inputs,
                    *(weights if c else [first]),
                    *[gathered[c][r] for r in range(1, wa)],
                    *adjoints,
                    *([] if c else parts),
                ],
                scalars=[turn, neighbours],
                scratch=scratch,
                flops=proj_flops,
            )
            if not c:
                later = after(info, dqkv, *[gathered[1][r] for r in GATE])
                odd = grads_of((1, 3), later, inputs, dqkv, rows_here)
                even = grads_of((0, 2), after(info, odd), inputs, dqkv, rows_here)
                got = swap(odd, "wa", wa, 1)
                passed = total_of(even, got, rows_here)
                owned = [even, got, swap(passed, "wa", wa, 2)]
                sent = [odd, even]
            else:
                shares = {}
                for r in (3, 1, 2, 0):
                    shares[r] = grads_of((r,), after(info, *shares.values()), inputs, dqkv, rows_here)
                ready.append(shares)
        else:
            cols = slice(c * LANES, (c + 1) * LANES)
            local = jnp.concatenate([w[:, cols] for w in weights], axis=1)
            panel = lax.all_gather(local, "wa", axis=0, tiled=True)
            dqkv = local_call(
                functools.partial(attention_panel_body, c, blocks),
                [shaped(nodes, 3 * LANES)],
                [inputs, panel, *adjoints],
                scalars=[turn, neighbours],
                scratch=scratch,
                flops=proj_flops,
            )[0]
            full = local_call(whole_grad_body, [shaped(width, 3 * LANES)], [inputs, dqkv])[0]
            owned.append(lax.psum_scatter(full, "wa", scatter_dimension=0, tiled=True))
        stacked.append(dqkv)
        panels.append(panel)

    if direct:
        (shares,) = ready
        message = swap(shares[3], "wa", wa, 1)
        sent = [shares[3]]
    backs = [
        local_call(
            functools.partial(back_body, range(odd, ta, 2), chunks),
            [shaped(nodes // 2, width)],
            [*stacked, *[after(p, *sent) for p in panels]],
        )[0]
        for odd in (1, 0)
    ]
    kept, got, early = scatter_halving(*backs, "ta", ta, nodes_here)
    if direct:
        wait = [owned[2]] + ([early] if early is not None else [])
        passed = total_of(shares[2], after(message, *wait), rows_here)
        direct_got = swap(after(shares[1], message), "wa", wa, 1)
        owned += [shares[0], direct_got, swap(passed, "wa", wa, 2)]
    if direct:
        *grads, back = local_call(
            functools.partial(join_body, chunks),
            [shaped(rows_here, columns)] * 3 + [shaped(nodes_here, width)],
            [*owned, kept, got],
            scalars=[info],
        )
    else:
        back = kept + got
        grads = [
            jnp.concatenate([o[:, i * LANES : (i + 1) * LANES] for o in owned], axis=1)
            for i in range(3)
        ]
    return (back[None], *grads)


def solution(mesh):
    sizes = tuple(mesh.shape[name] for name in ("grp", "wa", "ta"))
    return jax.shard_map(
        functools.partial(per_device, sizes),
        mesh=mesh,
        in_specs=(
            P(("grp", "wa"), "ta", None),
            P(("grp", "wa"), "ta", None),
            P("ta"),
            P(),
            P("wa", "ta"),
            P("wa", "ta"),
            P("wa", "ta"),
        ),
        out_specs=(
            P(("grp", "wa"), "ta", None),
            P(("grp", "wa"), "ta"),
            P(("grp", "wa"), "ta"),
            P(("grp", "wa"), "ta"),
        ),
        check_vma=False,
    )
```

```python
import functools

import jax
import jax.numpy as jnp
from jax import lax
from jax.experimental import pallas as pl
from jax.experimental.pallas import tpu as pltpu
from jax.sharding import PartitionSpec as P

DH = 64
BLOCK = 128
KB = 2
GATE = ()
LANES = 128
F32 = jnp.float32
NN = ((1,), (0,))
NT = ((1,), (1,))
TN = ((0,), (0,))


def dot(left, right, dims):
    return lax.dot_general(
        left, right, (dims, ((), ())), precision=lax.Precision.HIGHEST, preferred_element_type=F32
    )


def grads_of(shares, info, inputs, stacked, rows):
    return local_call(
        functools.partial(weight_grad_body, shares, rows),
        [shaped(rows * len(shares), stacked.shape[1])],
        [inputs, stacked],
        scalars=[info],
    )[0]


def total_of(kept, got, rows):
    return local_call(
        functools.partial(sum_body, rows), [shaped(rows, kept.shape[1])], [kept, got]
    )[0]


def local_call(body, outs, args, scalars=(), scratch=(), flops=0, vmem_mib=24):
    vmem = pl.BlockSpec(memory_space=pltpu.VMEM)
    smem = pl.BlockSpec(memory_space=pltpu.SMEM)
    return pl.pallas_call(
        body,
        out_shape=outs,
        in_specs=[smem] * len(scalars) + [vmem] * len(args),
        out_specs=[vmem] * len(outs),
        scratch_shapes=scratch,
        cost_estimate=pl.CostEstimate(flops=flops, bytes_accessed=flops // 256, transcendentals=0),
        compiler_params=pltpu.CompilerParams(vmem_limit_bytes=vmem_mib << 20),
    )(*scalars, *args)


def shaped(*shape):
    return jax.ShapeDtypeStruct(shape, F32)


def swap(value, axis, size, step):
    return lax.ppermute(value, axis, [(i, i ^ step) for i in range(size)])


def after(value, *others):
    return lax.optimization_barrier((value, *others))[0]


def entry_body(parts, ids, sensors, wq, wk, wv, packed, *refs):
    mine = lax.axis_index("ta")
    if packed is not None:
        packed[:, 0:LANES] = wq[...]
        packed[:, LANES : 2 * LANES] = wk[...]
        packed[:, 2 * LANES :] = wv[...]
    outs, rows = refs[:parts], refs[parts]
    count = sensors.shape[0]
    columns = outs[0].shape[1]
    local = ids[...] - mine * count
    chosen = lax.broadcasted_iota(jnp.int32, (count, count), 0) == local
    rows[...] = dot(chosen.astype(F32), sensors[...], NN)
    for r in range(parts):
        start = pl.multiple_of((mine ^ r) * columns, LANES)
        outs[r][...] = rows[:, pl.ds(start, columns)]


def entry(ids, sensors, weights, parts, direct):
    rows, columns = weights[0].shape
    count, width = sensors.shape

    def whole(*shape):
        return pl.BlockSpec(shape, lambda i: (0, 0))

    spec = pl.BlockSpec((rows, LANES), lambda i: (0, lax.axis_index("grp")))
    body = entry_body if direct else adjoint_body
    outs = ([(rows, 3 * LANES)] if direct else []) + [(count, columns)] * parts
    return pl.pallas_call(
        functools.partial(body, parts),
        out_shape=[shaped(*o) for o in outs],
        grid_spec=pltpu.PrefetchScalarGridSpec(
            num_scalar_prefetch=0,
            grid=(1,),
            in_specs=[whole(1, count), whole(count, width)] + ([spec] * 3 if direct else []),
            out_specs=[whole(*o) for o in outs],
            scratch_shapes=[pltpu.VMEM((count, width), F32)],
        ),
        compiler_params=pltpu.CompilerParams(vmem_limit_bytes=60 << 20),
    )(ids, sensors, *(weights if direct else ()))


def columns_of(turn, info):
    return pl.ds(pl.multiple_of((info[1] ^ turn) * LANES, LANES), LANES)


def spread(held, axis, size):
    held, step = dict(held), size
    while step > 1:
        step //= 2
        if step not in held:
            held.update({r | step: swap(v, axis, size, step) for r, v in list(held.items())})
    return held


def adjoint_body(parts, ids, sensors, *refs):
    entry_body(parts, ids, sensors, None, None, None, None, *refs)


def stack_body(parts, *refs):
    rows = refs[0].shape[0]
    for r in range(parts):
        refs[parts][r * rows : (r + 1) * rows, :] = refs[r][...]


def attention_body(turn, blocks, wa, info, neighbours, *refs):
    own = 1 if turn == 0 else 3
    x, *weights = refs[: 1 + own]
    pieces = refs[1 + own : own + wa]
    adjoints = refs[own + wa : own + wa + blocks]
    *parts, out, panel, proj = refs[own + wa + blocks :]
    cols = columns_of(turn, info)
    count = weights[0].shape[0]

    def rows(r):
        return pl.ds(pl.multiple_of((info[0] ^ r) * count, 8), count)

    if turn == 0:
        panel[rows(0), :] = weights[0][...]
    else:
        for i, weight in enumerate(weights):
            panel[rows(0), i * LANES : (i + 1) * LANES] = weight[:, cols]
    for r in range(1, wa):
        panel[rows(r), :] = pieces[r - 1][...]
    if parts:
        last = pl.ds(pl.multiple_of((info[0] ^ (wa - 1)) * count, LANES), count)
        proj[...] = parts[0][...] + dot(x[:, last], pieces[-1][...], NN)
    else:
        proj[...] = dot(x[...], panel[...], NN)
    attention_core(cols, blocks, info[2], neighbours, adjoints, out, proj)


def partial_body(info, x, *refs):
    *pieces, out = refs
    total = None
    for r, piece in enumerate(pieces):
        count = piece.shape[0]
        here = pl.ds(pl.multiple_of((info[0] ^ r) * count, LANES), count)
        term = dot(x[:, here], piece[...], NN)
        total = term if total is None else total + term
    out[...] = total


def attention_panel_body(chunk, blocks, info, neighbours, x, panel, *refs):
    cols = slice(chunk * LANES, (chunk + 1) * LANES)
    refs[blocks + 1][...] = dot(x[...], panel[...], NN)
    attention_core(cols, blocks, info[2], neighbours, refs[:blocks], *refs[blocks:])


BF16 = jnp.bfloat16


def halves_of(value):
    high = value.astype(BF16)
    return high, (value - high.astype(F32)).astype(BF16)


def dot_halves(left, right, dims):
    (high, low), (high_right, low_right) = left, right

    def term(one, other):
        return lax.dot_general(one, other, (dims, ((), ())), preferred_element_type=F32)

    return (term(high, low_right) + term(low, high_right)) + term(high, high_right)


def attention_core(cols, blocks, t, neighbours, adjoints, out, proj):
    out[:, LANES:] = jnp.zeros((out.shape[0], 2 * LANES), F32)
    first = lax.broadcasted_iota(jnp.int32, (BLOCK, LANES), 1) < DH
    scale = DH ** (-0.5)

    def by_head(value):
        return jnp.concatenate(
            [jnp.where(first, value, 0.0), jnp.where(first, 0.0, value)], axis=0
        )

    every = range(blocks)
    here = [slice(r * BLOCK, (r + 1) * BLOCK) for r in every]
    there = [
        [
            pl.ds(pl.multiple_of((neighbours[t ^ r, j] ^ t) * BLOCK, BLOCK), BLOCK)
            for j in range(KB)
        ]
        for r in every
    ]
    query = [by_head(proj[here[r], 0:LANES]) for r in every]
    adjoint = [by_head(adjoints[r][:, cols]) for r in every]
    key = [jnp.concatenate([proj[w, LANES : 2 * LANES] for w in there[r]], axis=0) for r in every]
    value = [jnp.concatenate([proj[w, 2 * LANES :] for w in there[r]], axis=0) for r in every]
    scores = [dot(query[r], key[r], NT) * scale for r in every]
    weight_adjoint = [dot(adjoint[r], value[r], NT) for r in every]
    raised = [jnp.exp(s - jnp.max(s, axis=1, keepdims=True)) for s in scores]
    attention = [v / jnp.sum(v, axis=1, keepdims=True) for v in raised]
    row_dots = [
        jnp.sum(attention[r] * weight_adjoint[r], axis=1, keepdims=True) for r in every
    ]
    score_adjoint = [
        halves_of(attention[r] * (weight_adjoint[r] - row_dots[r]) * scale) for r in every
    ]
    for r in every:
        dvalue = dot_halves(halves_of(attention[r]), halves_of(adjoint[r]), TN)
        both = dot_halves(score_adjoint[r], halves_of(key[r]), NN)
        out[here[r], 0:LANES] = jnp.where(first, both[:BLOCK], both[BLOCK:])
        dkey = dot_halves(score_adjoint[r], halves_of(query[r]), TN)
        for j, w in enumerate(there[r]):
            part = slice(j * BLOCK, (j + 1) * BLOCK)
            out[w, LANES : 2 * LANES] += dkey[part]
            out[w, 2 * LANES :] += dvalue[part]


def weight_grad_body(shares, rows, info, x, stacked, out):
    for j, r in enumerate(shares):
        start = pl.multiple_of((info[0] ^ r) * rows, LANES)
        out[j * rows : (j + 1) * rows, :] = dot_halves(
            halves_of(x[:, pl.ds(start, rows)]), halves_of(stacked[...]), TN
        )


def whole_grad_body(x, stacked, out):
    out[...] = dot(x[...], stacked[...], TN)


def back_body(shares, chunks, *refs):
    stacked, panels, out = refs[:chunks], refs[chunks : 2 * chunks], refs[2 * chunks]
    total = None
    for c in range(chunks):
        rows = jnp.concatenate(
            [stacked[c][r * BLOCK : (r + 1) * BLOCK, :] for r in shares], axis=0
        )
        term = dot(rows, panels[c][...], NT)
        total = term if total is None else total + term
    out[...] = total


def halve_body(rows, keep, got, send, kept):
    for j in range(keep.shape[0] // rows):
        out = send if j % 2 else kept
        place = slice(j // 2 * rows, (j // 2 + 1) * rows)
        here = slice(j * rows, (j + 1) * rows)
        out[place, :] = keep[here, :] + got[here, :]


def scatter_halving(send, keep, axis, size, rows):
    step, first = 1, None
    while True:
        got = swap(send, axis, size, step)
        step *= 2
        if step == size:
            return keep, got, first
        shape = shaped(keep.shape[0] // 2, keep.shape[1])
        send, keep = local_call(functools.partial(halve_body, rows), [shape] * 2, [keep, got])
        first = keep if first is None else first


def sum_body(rows, kept, got, out):
    out[...] = kept[-rows:, :] + got[-rows:, :]


def join_body(turns, info, *refs):
    *refs, back = refs
    count = (len(refs) - 5) // turns
    back[...] = refs[turns * count][...] + refs[turns * count + 1][...]
    outs = refs[turns * count + 2 :]
    for turn in range(turns):
        for i in range(3):
            part = slice(i * LANES, (i + 1) * LANES)
            rows = outs[0].shape[0]
            total = refs[turn * count][:rows, part]
            for term in refs[turn * count + 1 : (turn + 1) * count]:
                total += term[:rows, part]
            outs[i][:, columns_of(turn, info)] = total


def per_device(sizes, node_features, sensor_adjoint, sensor_node, neighbours, *weights):
    grp, wa, ta = sizes
    hour_rows = node_features[0]
    nodes_here, width = hour_rows.shape
    rows_here, columns = weights[0].shape
    chunks = columns // LANES
    blocks = ta
    nodes = nodes_here * ta
    z, y, t = lax.axis_index("wa"), lax.axis_index("grp"), lax.axis_index("ta")
    info = jnp.stack([z, y, t]).astype(jnp.int32)
    direct = rows_here % LANES == 0 and chunks == grp == 2 and wa == 4

    blocks_out = entry(sensor_node.reshape(1, -1), sensor_adjoint[0], weights, ta, direct)
    held = {0: hour_rows}
    if direct:
        first, *blocks_out = blocks_out
        held[0] = after(hour_rows, first)
        gathered = [spread({0: first}, "wa", wa)]
        gathered.append({1: swap(gathered[0][1], "grp", grp, 1)})
        held[ta // 2] = after(swap(held[0], "ta", ta, ta // 2), gathered[0][1])
    held = spread(held, "ta", ta)
    adjoints = [blocks_out[0]] + [
        swap(after(blocks_out[r], *[held[q] for q in range(1, ta)]), "ta", ta, r) for r in range(1, ta)
    ]
    inputs = local_call(
        functools.partial(stack_body, ta), [shaped(nodes, width)], [held[r] for r in range(ta)]
    )[0]

    parts = []
    if direct:
        parts = local_call(
            partial_body,
            [shaped(nodes, 3 * LANES)],
            [inputs, *[gathered[0][r] for r in range(wa - 1)]],
            scalars=[info],
        )
        gathered[1][2] = swap(after(gathered[0][2], *parts, gathered[1][1]), "grp", grp, 1)
        gathered[1][3] = swap(gathered[0][3], "grp", grp, 1)

    stacked, panels, owned, sent, ready = [], [], [], [], []
    for c in range(chunks):
        proj_flops = 12 * nodes * width * 3 * LANES + 60 * 2 * nodes * 4 * BLOCK * LANES
        scratch = [pltpu.VMEM((nodes, 3 * LANES), F32)]
        turn = after(info, stacked[-1], *sent) if stacked else info
        if direct:
            dqkv, panel = local_call(
                functools.partial(attention_body, c, blocks, wa),
                [shaped(nodes, 3 * LANES), shaped(width, 3 * LANES)],
                [
                    inputs,
                    *(weights if c else [first]),
                    *[gathered[c][r] for r in range(1, wa)],
                    *adjoints,
                    *([] if c else parts),
                ],
                scalars=[turn, neighbours],
                scratch=scratch,
                flops=proj_flops,
            )
            if not c:
                later = after(info, dqkv, *[gathered[1][r] for r in GATE])
                odd = grads_of((1, 3), later, inputs, dqkv, rows_here)
                even = grads_of((0, 2), after(info, odd), inputs, dqkv, rows_here)
                got = swap(odd, "wa", wa, 1)
                passed = total_of(even, got, rows_here)
                owned = [even, got, swap(passed, "wa", wa, 2)]
                sent = [odd, even]
            else:
                shares = {}
                for r in (3, 1, 2, 0):
                    shares[r] = grads_of((r,), after(info, *shares.values()), inputs, dqkv, rows_here)
                ready.append(shares)
        else:
            cols = slice(c * LANES, (c + 1) * LANES)
            local = jnp.concatenate([w[:, cols] for w in weights], axis=1)
            panel = lax.all_gather(local, "wa", axis=0, tiled=True)
            dqkv = local_call(
                functools.partial(attention_panel_body, c, blocks),
                [shaped(nodes, 3 * LANES)],
                [inputs, panel, *adjoints],
                scalars=[turn, neighbours],
                scratch=scratch,
                flops=proj_flops,
            )[0]
            full = local_call(whole_grad_body, [shaped(width, 3 * LANES)], [inputs, dqkv])[0]
            owned.append(lax.psum_scatter(full, "wa", scatter_dimension=0, tiled=True))
        stacked.append(dqkv)
        panels.append(panel)

    if direct:
        (shares,) = ready
        message = swap(shares[3], "wa", wa, 1)
        sent = [shares[3]]
    backs = [
        local_call(
            functools.partial(back_body, range(odd, ta, 2), chunks),
            [shaped(nodes // 2, width)],
            [*stacked, *[after(p, *sent) for p in panels]],
        )[0]
        for odd in (1, 0)
    ]
    kept, got, early = scatter_halving(*backs, "ta", ta, nodes_here)
    if direct:
        wait = [owned[2]] + ([early] if early is not None else [])
        passed = total_of(shares[2], after(message, *wait), rows_here)
        direct_got = swap(after(shares[1], message), "wa", wa, 1)
        owned += [shares[0], direct_got, swap(passed, "wa", wa, 2)]
    if direct:
        *grads, back = local_call(
            functools.partial(join_body, chunks),
            [shaped(rows_here, columns)] * 3 + [shaped(nodes_here, width)],
            [*owned, kept, got],
            scalars=[info],
        )
    else:
        back = kept + got
        grads = [
            jnp.concatenate([o[:, i * LANES : (i + 1) * LANES] for o in owned], axis=1)
            for i in range(3)
        ]
    return (back[None], *grads)


def solution(mesh):
    sizes = tuple(mesh.shape[name] for name in ("grp", "wa", "ta"))
    return jax.shard_map(
        functools.partial(per_device, sizes),
        mesh=mesh,
        in_specs=(
            P(("grp", "wa"), "ta", None),
            P(("grp", "wa"), "ta", None),
            P("ta"),
            P(),
            P("wa", "ta"),
            P("wa", "ta"),
            P("wa", "ta"),
        ),
        out_specs=(
            P(("grp", "wa"), "ta", None),
            P(("grp", "wa"), "ta"),
            P(("grp", "wa"), "ta"),
            P(("grp", "wa"), "ta"),
        ),
        check_vma=False,
    )
```
